512 devices in a mesh: seq: 128 (over z, y, core), tp: 4 (over x).
Axes of the slice: x: 4, y: 8, z: 8, core: 2. Of those that a mesh axis runs over, the one named last changes fastest.
Arguments:
- queries: bfloat16 [32768, 4096], P('seq', 'tp'), may hold values from -6 to 6, as said below
- keys: bfloat16 [32768, 512], P('seq', 'tp'), may hold values from -6 to 6, as said below
- values: bfloat16 [32768, 512], P('seq', 'tp'), may hold values from -6 to 6
- segment: int32 [32768], P('seq'), may hold values from 0 to 255, never falling along the last dimension, each value on 1 to 512 neighbouring positions
- repack: int32 [32768], P('seq'), may hold values from 0 to 32767, as said below
- proj: bfloat16 [1536, 4096], P('seq', 'tp'), may hold values from -0.5 to 0.5
- student_states: bfloat16 [32768, 1536], P('seq'), may hold values from -6 to 6
- target_row: int32 [32768], P('seq'), may hold values from 0 to 255
Outputs:
- student_rows: bfloat16 [32768, 1536], P('seq', 'tp')
- grad: float32 [1536, 4096], P('seq', 'tp')
The draws below stay inside these ranges and needn't reach their ends.
Inputs may be any that keep to these rules, and one draw needn't show every extreme that they name: `queries`: scaled normal entries. `keys`: scaled normal entries. `repack`: A permutation of the student rows. Each device's teacher rows go in consecutive groups of 4 rows, in order, each group to one student owner (the device holding student rows owner * 256 to owner * 256 + 255); every device sends exactly 4 rows to each of 64 other devices and none to itself, so at most 4 rows from one device to one owner, reached by every sending pair.
All inputs are finite; a program needn't handle non-finite values.
Results may differ from the reference program's by a relative error of at most 0.0056.
Values may be sent and summed in bfloat16 or wider, within the bound.
No kernel may reach another device: no remote copies, remote signals or barrier semaphores. Data moves between devices by JAX's collectives and lax.ppermute only.
A program may use at most 64 MiB of HBM per device.

```python
import math
import jax
import jax.numpy as jnp
import numpy as np
from jax import lax

HEADS = 32
KV_HEADS = 4
HEAD_DIM = 128
SW = 1536
TOK_DEV = 256
REACH = 2
TOKENS = 32768
MOST_DOC = 512
DOCS = 256
CAP = 4


def draw_queries(key, part):
    base = jax.random.normal(jax.random.fold_in(key, 1), (TOKENS, HEADS, HEAD_DIM), jnp.float32)
    base = jnp.clip(base, -6.0, 6.0)
    return base.reshape(TOKENS, HEADS * HEAD_DIM).astype(jnp.bfloat16)


def draw_keys(key, part):
    base = jax.random.normal(jax.random.fold_in(key, 2), (TOKENS, KV_HEADS, HEAD_DIM), jnp.float32)
    base = jnp.clip(base, -6.0, 6.0)
    return base.reshape(TOKENS, KV_HEADS * HEAD_DIM).astype(jnp.bfloat16)


def draw_repack(key, part):
    groups = TOK_DEV // CAP
    senders = TOKENS // TOK_DEV
    offsets = jax.random.permutation(jax.random.fold_in(key, 11), senders - 1)[:groups] + 1

    def per_source(source):
        order = jax.random.permutation(jax.random.fold_in(jax.random.fold_in(key, 12), source), groups)
        owner = (source + offsets[order]) % senders
        group_rows = owner * TOK_DEV + order * CAP
        return (group_rows[:, None] + jnp.arange(CAP)[None, :]).reshape(-1)
    return jax.vmap(per_source)(jnp.arange(senders)).reshape(-1).astype(jnp.int32)


def plant(entries, stream_key, least, high):
    longest = entries.shape.index(max(entries.shape))
    spots = []
    for shift in (0, 1):
        where = [jax.random.randint(jax.random.fold_in(stream_key, axis), (), 0, length) for axis, length in enumerate(entries.shape)]
        where[longest] = (where[longest] + shift) % entries.shape[longest]
        spots.append(tuple(where))
    return entries.at[spots[0]].set(least).at[spots[1]].set(high)


def level_of(key, extent, shards, low, largest):
    def one(dim, shards_of):
        steps = jax.random.uniform(jax.random.fold_in(jax.random.fold_in(key, 6), dim), (shards_of,), jnp.float32, low / len(shards), largest / len(shards))
        return jnp.repeat(jnp.exp(steps), extent[dim] // shards_of).reshape((-1,) + (1,) * (len(extent) - dim - 1))

    factor_of = one(*shards[0])
    for cut in shards[1:]:
        factor_of = factor_of * one(*cut)
    return factor_of


def split_up(amount, total, limit, slope):
    portions = [(1 << 20) // math.isqrt(grade ** slope) + 1 for grade in range(2, amount + 1)]
    spare, counts = total - limit - (amount - 1), [1] * (amount - 1)
    while spare > 0:
        movable = [i for i in range(amount - 1) if counts[i] < limit]
        whole, remaining = sum([portions[i] for i in movable]), spare
        for i in movable:
            more = min(limit - counts[i], max(1, remaining * portions[i] // whole), spare)
            counts[i] = counts[i] + more
            spare = spare - more
    return np.array([limit] + counts)


def ragged_sizes(rng, count, total, reach, lean):
    if count == 2:
        one = jax.random.randint(rng, (), max(1, total - reach), min(reach, total - 1) + 1)
        return jnp.stack([one, total - one])
    lengths = jnp.asarray(split_up(count, total, reach, lean), jnp.int32)
    pairs = (count - 1) // 2
    donor, receiver = lengths[1:1 + 2 * pairs:2], lengths[2:2 + 2 * pairs:2]
    slack = jnp.minimum(donor - 1, reach - receiver)
    moved = jax.random.randint(jax.random.fold_in(rng, 1), (pairs,), 0, 1 << 20) % (slack + 1)
    lengths = lengths.at[1:1 + 2 * pairs:2].set(donor - moved).at[2:2 + 2 * pairs:2].set(receiver + moved)
    return lengths[jax.random.permutation(jax.random.fold_in(rng, 2), count)]


def gaussian(own_key, extent, spread, limit, cuts=(), held_as=jnp.bfloat16):
    level = level_of(own_key, extent, cuts, -0.22, 0.18) if cuts else 1.0
    result = jax.random.normal(own_key, extent, jnp.float32) * spread * level
    return jnp.minimum(jnp.maximum(result, -limit), limit).astype(held_as)


def setup_inputs(seed: int = 0) -> dict:
    splits = jax.random.split(jax.random.key(seed), 9)
    queries = draw_queries(jax.random.fold_in(splits[8], 71), 0)
    keys = draw_keys(jax.random.fold_in(splits[8], 71), 0)
    values = gaussian(splits[2], (TOKENS, KV_HEADS * HEAD_DIM), 1.0, 6.0, ((0, 128), (1, 4)))
    segment = jnp.searchsorted(jnp.cumsum(ragged_sizes(splits[3], DOCS, TOKENS, MOST_DOC, 2)), jnp.arange(TOKENS), side="right").astype(jnp.int32)
    repack = draw_repack(jax.random.fold_in(splits[8], 71), 0)
    proj = gaussian(splits[5], (SW, HEADS * HEAD_DIM), HEAD_DIM ** -0.5, 0.5, ((0, 128), (1, 4)))
    student_states = gaussian(splits[6], (TOKENS, SW), 1.0, 6.0, ((0, 128),))
    target_row = plant(jax.random.randint(splits[7], (TOKENS,), 0, TOK_DEV), jax.random.fold_in(splits[7], 1), 0, TOK_DEV - 1).astype(jnp.int32)
    return {"queries": queries, "keys": keys, "values": values, "segment": segment, "repack": repack, "proj": proj, "student_states": student_states, "target_row": target_row}


def document_attention(queries, keys, values, segment):
    group = HEADS // KV_HEADS
    pad_rows = REACH * TOK_DEV
    span = pad_rows + TOK_DEV
    keys_pad = jnp.concatenate([jnp.zeros((pad_rows, keys.shape[1]), keys.dtype), keys], 0)
    values_pad = jnp.concatenate([jnp.zeros((pad_rows, values.shape[1]), values.dtype), values], 0)
    segment_pad = jnp.concatenate([jnp.full((pad_rows,), -1, jnp.int32), segment.astype(jnp.int32)], 0)
    scale = 1.0 / math.sqrt(HEAD_DIM)

    def one_block(index):
        first = (index * TOK_DEV).astype(jnp.int32)
        query_rows = lax.dynamic_slice_in_dim(queries, first, TOK_DEV, 0)
        key_rows = lax.dynamic_slice_in_dim(keys_pad, first, span, 0)
        value_rows = lax.dynamic_slice_in_dim(values_pad, first, span, 0)
        query_seg = lax.dynamic_slice_in_dim(segment.astype(jnp.int32), first, TOK_DEV, 0)
        key_seg = lax.dynamic_slice_in_dim(segment_pad, first, span, 0)
        query_pos = first + jnp.arange(TOK_DEV, dtype=jnp.int32)
        key_pos = first - pad_rows + jnp.arange(span, dtype=jnp.int32)
        allowed = (query_seg[:, None] == key_seg[None, :]) & (key_pos[None, :] <= query_pos[:, None])
        q_heads = query_rows.reshape(TOK_DEV, KV_HEADS, group, HEAD_DIM).astype(jnp.float32)
        k_heads = key_rows.reshape(span, KV_HEADS, HEAD_DIM).astype(jnp.float32)
        v_heads = value_rows.reshape(span, KV_HEADS, HEAD_DIM).astype(jnp.float32)
        scores = jnp.einsum('tgjd,sgd->gjts', q_heads, k_heads) * scale
        scores = jnp.where(allowed[None, None], scores, -1e+30)
        top = lax.optimization_barrier(jnp.max(scores, axis=-1, keepdims=True))
        expo = jnp.exp(scores - top)
        weights = (expo / lax.optimization_barrier(jnp.sum(expo, axis=-1, keepdims=True))).astype(jnp.bfloat16)
        mixed = jnp.einsum('gjts,sgd->tgjd', weights.astype(jnp.float32), v_heads)
        return mixed.reshape(TOK_DEV, HEADS * HEAD_DIM).astype(jnp.bfloat16)
    blocks = lax.map(one_block, jnp.arange(TOKENS // TOK_DEV, dtype=jnp.int32))
    return blocks.reshape(TOKENS, HEADS * HEAD_DIM)

def reference(queries, keys, values, segment, repack, proj, student_states, target_row):
    attended = document_attention(queries, keys, values, segment)
    moved = jnp.zeros_like(attended).at[repack.astype(jnp.int32)].set(attended)
    student_full = jnp.dot(moved, proj.T, preferred_element_type=jnp.float32)
    student_rows = student_full.astype(jnp.bfloat16)
    base_row = jnp.arange(TOKENS, dtype=jnp.int32) // TOK_DEV * TOK_DEV
    target = student_states[base_row + target_row.astype(jnp.int32)]
    delta = (student_rows.astype(jnp.float32) - target.astype(jnp.float32)).astype(jnp.bfloat16)
    grad = jnp.dot(delta.T, moved, preferred_element_type=jnp.float32) * (1.0 / math.sqrt(TOKENS))
    return (student_rows, grad)
```

```python
import math

import jax
import jax.numpy as jnp
from jax import lax
from jax.sharding import PartitionSpec as P

HEADS = 32
KV_HEADS = 4
HEAD_DIM = 128
SW = 1536
REACH = 2
GROUP_ROWS = 4


neg_large = -1e30


def passed_along(block, axis, distance):
    devices = range(lax.axis_size(axis))
    route = [(i - distance, i) for i in devices if i - distance in devices]
    return lax.ppermute(block, axis, route)


def attend(queries, keys, values, segment):
    row_count = queries.shape[0]
    lanes = keys.shape[1]
    seg_rows = (segment + 1).astype(jnp.bfloat16).reshape(-1, lanes)
    seg_rows = jnp.concatenate([seg_rows, jnp.zeros((14, lanes), jnp.bfloat16)], 0)
    packed = jnp.concatenate([keys, values, seg_rows], 0)
    blocks = [packed]
    for step in range(1, REACH + 1):
        blocks.insert(0, passed_along(packed, "seq", step))
    all_keys = jnp.concatenate([b[:row_count] for b in blocks], 0)
    all_values = jnp.concatenate([b[row_count : 2 * row_count] for b in blocks], 0)
    key_seg = jnp.concatenate(
        [b[2 * row_count : 2 * row_count + 2].reshape(-1) for b in blocks], 0
    ).astype(jnp.int32)
    key_pos = jnp.arange(3 * row_count, dtype=jnp.int32) - REACH * row_count
    row_pos = jnp.arange(row_count, dtype=jnp.int32)
    allowed = (key_seg[None, :] == (segment + 1)[:, None]) & (key_pos[None, :] <= row_pos[:, None])
    group = HEADS // KV_HEADS
    q_heads = queries.reshape(row_count, group, HEAD_DIM)
    scale = 1.0 / math.sqrt(HEAD_DIM)
    outputs = []
    for head in range(group):
        scores = (
            jnp.einsum("td,sd->ts", q_heads[:, head], all_keys, preferred_element_type=jnp.float32)
            * scale
        )
        scores = jnp.where(allowed, scores, neg_large)
        top = jnp.max(scores, axis=-1, keepdims=True)
        expo = jnp.exp(scores - top)
        weights = (expo / jnp.sum(expo, axis=-1, keepdims=True)).astype(jnp.bfloat16)
        mixed = jnp.einsum("ts,sd->td", weights, all_values, preferred_element_type=jnp.float32)
        outputs.append(mixed.astype(jnp.bfloat16))
    return jnp.concatenate(outputs, axis=1)


def on_device(queries, keys, values, segment, repack, proj, student_states, target_row):
    row_count = queries.shape[0]
    devices = lax.axis_size("seq")
    groups = row_count // GROUP_ROWS
    attended = attend(queries, keys, values, segment)
    target_dev = repack // row_count
    local_slot = repack - target_dev * row_count
    owners = target_dev.reshape(groups, GROUP_ROWS)[:, 0]
    owner_hot = owners[None, :] == jnp.arange(devices, dtype=jnp.int32)[:, None]
    slots_by_group = local_slot.reshape(groups, GROUP_ROWS)
    slot_table = jnp.sum(
        jnp.where(owner_hot[:, :, None], slots_by_group[None], 0), axis=1
    )
    slot_table = jnp.where(jnp.any(owner_hot, axis=1)[:, None], slot_table, row_count)
    slots = lax.all_to_all(slot_table, "seq", split_axis=0, concat_axis=0, tiled=True)
    width_share = SW // lax.axis_size("tp")
    tp_index = lax.axis_index("tp")
    targets = student_states[target_row]
    bucket_dev = jnp.arange(devices * GROUP_ROWS, dtype=jnp.int32) // GROUP_ROWS
    bucket_pos = jnp.arange(devices * GROUP_ROWS, dtype=jnp.int32) % GROUP_ROWS
    row_ids = jnp.arange(row_count, dtype=jnp.int32)
    pick = (
        (bucket_dev[:, None] == target_dev[None, :])
        & (bucket_pos[:, None] == (row_ids % GROUP_ROWS)[None, :])
    ).astype(jnp.bfloat16)
    buckets = jnp.dot(pick, attended, preferred_element_type=jnp.float32).astype(jnp.bfloat16)
    arrived = lax.all_to_all(buckets, "seq", split_axis=0, concat_axis=0, tiled=True)
    place = (row_ids[:, None] == slots.reshape(-1)[None, :]).astype(jnp.bfloat16)
    student_x = jnp.dot(place, arrived, preferred_element_type=jnp.float32).astype(jnp.bfloat16)
    all_proj = lax.all_gather(proj, "seq", axis=0, tiled=True)
    y_part = jnp.einsum("tf,nf->tn", student_x, all_proj, preferred_element_type=jnp.float32)
    y_total = lax.psum(y_part, "tp")
    y_rounded = y_total.astype(jnp.bfloat16)
    delta = (y_rounded.astype(jnp.float32) - targets.astype(jnp.float32)).astype(jnp.bfloat16)
    out_rows = lax.dynamic_slice_in_dim(y_rounded, tp_index * width_share, width_share, 1)
    norm_factor = 1.0 / math.sqrt(row_count * devices)
    grad_rows = delta.shape[1] // devices
    term = jnp.einsum("ts,tf->sf", delta, student_x, preferred_element_type=jnp.float32)
    pieces = term.reshape(devices, grad_rows, term.shape[1])
    summed = lax.all_to_all(
        pieces.astype(jnp.bfloat16), "seq", split_axis=0, concat_axis=0, tiled=True
    ).astype(pieces.dtype)
    grad = jnp.sum(summed, axis=0) * norm_factor
    return (out_rows, grad)


def solution(mesh):
    placed = (
        P("seq", "tp"),
        P("seq", "tp"),
        P("seq", "tp"),
        P("seq"),
        P("seq"),
        P("seq", "tp"),
        P("seq", None),
        P("seq"),
    )
    return jax.shard_map(
        on_device,
        mesh=mesh,
        in_specs=placed,
        out_specs=(P("seq", "tp"), P("seq", "tp")),
        check_vma=False,
    )
```

```python
import math

import jax
import jax.numpy as jnp
from jax import lax
from jax.sharding import PartitionSpec as P

HEADS = 32
KV_HEADS = 4
HEAD_DIM = 128
SW = 1536
REACH = 2
GROUP_ROWS = 4
SIDE = 8

neg_large = -1e30
bf16, f32, i32 = jnp.bfloat16, jnp.float32, jnp.int32


def seq_index(z, y, core):
    return (z * SIDE + y) * 2 + core


NEAR = [[seq_index(z, y, 0) for y in range(SIDE)] for z in range(SIDE)] + [
    [seq_index(z, y, 1) for z in range(SIDE)] for y in range(SIDE)
]
FAR = [[seq_index(z, y, 0) for z in range(SIDE)] for y in range(SIDE)] + [
    [seq_index(z, y, 1) for y in range(SIDE)] for z in range(SIDE)
]


def exchange(block, groups=None, axis="seq"):
    return lax.all_to_all(
        block, axis, split_axis=0, concat_axis=0, tiled=True, axis_index_groups=groups
    )


def passed_along(block, axis, distance):
    devices = range(lax.axis_size(axis))
    route = [(i - distance, i) for i in devices if i - distance in devices]
    return lax.ppermute(block, axis, route)


def other_core(block):
    return lax.ppermute(block, "seq", [(i, i ^ 1) for i in range(lax.axis_size("seq"))])


def to_all(block, count):
    return jnp.broadcast_to(block[None], (count,) + block.shape)


def attend(queries, keys, values, segment):
    row_count = queries.shape[0]
    lanes = keys.shape[1]
    seg_rows = (segment + 1).astype(bf16).reshape(-1, lanes)
    seg_rows = jnp.concatenate([seg_rows, jnp.zeros((14, lanes), bf16)], 0)
    packed = jnp.concatenate([keys, values, seg_rows], 0)
    blocks = [packed]
    for step in range(1, REACH + 1):
        blocks.insert(0, passed_along(packed, "seq", step))
    all_keys = jnp.concatenate([b[:row_count] for b in blocks], 0)
    all_values = jnp.concatenate([b[row_count : 2 * row_count] for b in blocks], 0)
    key_seg = jnp.concatenate(
        [b[2 * row_count : 2 * row_count + 2].reshape(-1) for b in blocks], 0
    ).astype(i32)
    key_pos = jnp.arange(3 * row_count, dtype=i32) - REACH * row_count
    row_pos = jnp.arange(row_count, dtype=i32)
    allowed = (key_seg[None, :] == (segment + 1)[:, None]) & (key_pos[None, :] <= row_pos[:, None])
    group = HEADS // KV_HEADS
    q_heads = queries.reshape(row_count, group, HEAD_DIM)
    scale = 1.0 / math.sqrt(HEAD_DIM)
    outputs = []
    for head in range(group):
        scores = (
            jnp.einsum("td,sd->ts", q_heads[:, head], all_keys, preferred_element_type=f32)
            * scale
        )
        scores = jnp.where(allowed, scores, neg_large)
        top = jnp.max(scores, axis=-1, keepdims=True)
        expo = jnp.exp(scores - top)
        weights = (expo / jnp.sum(expo, axis=-1, keepdims=True)).astype(bf16)
        mixed = jnp.einsum("ts,sd->td", weights, all_values, preferred_element_type=f32)
        outputs.append(mixed.astype(bf16))
    return jnp.concatenate(outputs, axis=1)


def dot(a, b, dims):
    return lax.dot_general(a, b, (dims, ((), ())), preferred_element_type=f32)


def hot(a, b):
    return (a == b).astype(bf16)


def spread_of(core):
    block = jnp.arange(192, dtype=i32) // 12
    inner = jnp.arange(192, dtype=i32) % 12
    if core == 0:
        pair = block
    else:
        pair = (block % 2) * SIDE + block // 2
    source = 24 * pair + 12 * core + inner
    return hot(jnp.arange(384, dtype=i32)[:, None], source[None, :])


def on_device(queries, keys, values, segment, repack, proj, student_states, target_row):
    rows = queries.shape[0]
    devices = lax.axis_size("seq")
    shares = lax.axis_size("tp")
    groups = rows // GROUP_ROWS
    share = SW // shares
    core = lax.axis_index("seq") % 2
    tp_index = lax.axis_index("tp")
    feats = proj.shape[0]
    near = exchange(to_all(proj, SIDE), NEAR)
    near = near.reshape(SIDE * feats, -1)
    half_proj = exchange(to_all(near, SIDE), FAR).reshape(SIDE * SIDE * feats, -1)
    target_dev = repack // rows
    local_slot = repack - target_dev * rows
    owners = target_dev.reshape(groups, GROUP_ROWS)[:, 0]
    owner_hot = owners[None, :] == jnp.arange(devices, dtype=i32)[:, None]
    slots_by_group = local_slot.reshape(groups, GROUP_ROWS)
    slot_table = jnp.sum(jnp.where(owner_hot[:, :, None], slots_by_group[None], 0), axis=1)
    slot_table = jnp.where(jnp.any(owner_hot, axis=1)[:, None], slot_table, rows)
    slots = exchange(slot_table).reshape(-1)
    slot_hot = hot(slots[:, None], jnp.arange(rows, dtype=i32)[None, :])
    student_part = lax.dynamic_slice_in_dim(student_states, tp_index * share, share, 1)
    chosen = dot(hot(target_row[:, None], jnp.arange(rows, dtype=i32)[None, :]), student_part, ((1,), (0,)))
    chosen = dot(slot_hot, chosen.astype(bf16), ((1,), (0,))).astype(bf16)
    spreads = [spread_of(0), spread_of(1)]
    chips = devices // 2
    outgoing = [
        dot(chosen, s, ((1,), (0,))).astype(bf16).reshape(chips, 1, 2 * GROUP_ROWS, -1)
        for s in spreads
    ]
    outgoing = jnp.concatenate(outgoing, 1).reshape(devices, 2 * GROUP_ROWS, -1)
    target_in = exchange(outgoing).reshape(devices * 2 * GROUP_ROWS, -1)
    dev_both = jnp.concatenate([target_dev, other_core(target_dev)], 0)
    row_ids = jnp.arange(2 * rows, dtype=i32)
    row_core = jnp.where(row_ids < rows, core, 1 - core)
    row_place = dev_both * (2 * GROUP_ROWS) + row_core * GROUP_ROWS + row_ids % GROUP_ROWS
    place_hot = hot(jnp.arange(devices * 2 * GROUP_ROWS, dtype=i32)[:, None], row_place[None, :])
    target = dot(target_in, place_hot, ((0,), (0,)))
    attended = attend(queries, keys, values, segment)
    both = jnp.concatenate([attended, other_core(attended)], 0)
    y_part = dot(half_proj, both, ((1,), (1,))).astype(bf16)
    per_share = y_part.shape[0] // shares
    along = y_part.reshape(shares, per_share, 2 * rows)
    across = y_part.reshape(SIDE, shares, 2 * feats, 2 * rows).swapaxes(0, 1)
    y_split = jnp.where(core == 0, along, across.reshape(along.shape))
    y_terms = exchange(y_split, axis="tp")
    y_rounded = jnp.sum(y_terms.astype(f32), axis=0).astype(bf16)
    delta = (y_rounded.astype(f32) - target).astype(bf16)
    deltas = exchange(to_all(delta, shares), axis="tp")
    y_out = dot(place_hot, y_rounded, ((1,), (1,))).astype(bf16)
    y_in = exchange(y_out.reshape(devices, 2 * GROUP_ROWS, -1))
    y_in = y_in.reshape(chips, 2, 2 * GROUP_ROWS, -1)
    out_rows = 0.0
    for k in range(2):
        part = y_in[:, k].reshape(chips * 2 * GROUP_ROWS, -1)
        part = dot(slot_hot, part, ((0,), (0,))).astype(bf16)
        out_rows = out_rows + dot(part, spreads[k], ((1,), (1,)))
    out_rows = out_rows.astype(bf16)
    across = deltas.reshape(shares, SIDE, 2 * feats, 2 * rows).swapaxes(0, 1)
    deltas = jnp.where(
        core == 0, deltas.reshape(-1, 2 * rows), across.reshape(-1, 2 * rows)
    )
    term = dot(deltas, both, ((1,), (0,))).astype(bf16)
    far = exchange(term.reshape(SIDE, SIDE * feats, -1), FAR)
    far = jnp.sum(far.astype(f32), axis=0).astype(bf16)
    last = exchange(far.reshape(SIDE, feats, -1), NEAR)
    norm_factor = 1.0 / math.sqrt(rows * devices)
    grad = jnp.sum(last.astype(f32), axis=0) * norm_factor
    return (out_rows, grad)


def solution(mesh):
    placed = (
        P("seq", "tp"),
        P("seq", "tp"),
        P("seq", "tp"),
        P("seq"),
        P("seq"),
        P("seq", "tp"),
        P("seq", None),
        P("seq"),
    )
    return jax.shard_map(
        on_device,
        mesh=mesh,
        in_specs=placed,
        out_specs=(P("seq", "tp"), P("seq", "tp")),
        check_vma=False,
    )
```

```python
import math

import jax
import jax.numpy as jnp
from jax import lax
from jax.experimental import pallas as pl
from jax.experimental.pallas import tpu as pltpu
from jax.sharding import PartitionSpec as P


HEADS = 32
KV_HEADS = 4
HEAD_DIM = 128
SW = 1536
REACH = 2
GROUP_ROWS = 4
SIDE = 8

neg_large = -1e30
bf16, f32, i32 = jnp.bfloat16, jnp.float32, jnp.int32


def seq_index(z, y, core):
    return (z * SIDE + y) * 2 + core


NEAR = [[seq_index(z, y, 0) for y in range(SIDE)] for z in range(SIDE)] + [
    [seq_index(z, y, 1) for z in range(SIDE)] for y in range(SIDE)
]
FAR = [[seq_index(z, y, 0) for z in range(SIDE)] for y in range(SIDE)] + [
    [seq_index(z, y, 1) for y in range(SIDE)] for z in range(SIDE)
]


def exchange(block, groups=None, axis="seq"):
    return lax.all_to_all(
        block, axis, split_axis=0, concat_axis=0, tiled=True, axis_index_groups=groups
    )


def passed_along(block, axis, distance):
    devices = range(lax.axis_size(axis))
    route = [(i - distance, i) for i in devices if i - distance in devices]
    return lax.ppermute(block, axis, route)


def along_ring(block, distance):
    route = []
    for z in range(SIDE):
        for y in range(SIDE):
            route.append((seq_index(z, y, 0), seq_index((z + distance) % SIDE, y, 0)))
            route.append((seq_index(z, y, 1), seq_index(z, (y + distance) % SIDE, 1)))
    return lax.ppermute(block, "seq", route)


def other_core(block):
    return lax.ppermute(block, "seq", [(i, i ^ 1) for i in range(lax.axis_size("seq"))])


def to_all(block, count):
    return jnp.broadcast_to(block[None], (count,) + block.shape)


def attend_kernel(q_ref, b2_ref, b1_ref, b0_ref, o_ref, bias_ref):
    rows = q_ref.shape[0]
    blocks = (b2_ref, b1_ref, b0_ref)
    seg_lanes = [
        b[2 * rows + i : 2 * rows + i + 1, :].astype(f32) for b in blocks for i in range(2)
    ]
    seg_keys = jnp.concatenate(seg_lanes, axis=1)
    for i in range(2):
        column = jnp.transpose(jnp.broadcast_to(seg_lanes[4 + i], (HEAD_DIM, HEAD_DIM)))
        column = jnp.concatenate([column] * 6, axis=1)
        row_pos = lax.broadcasted_iota(i32, column.shape, 0) + i * HEAD_DIM
        key_pos = lax.broadcasted_iota(i32, column.shape, 1) - REACH * rows
        allowed = (column == seg_keys) & (key_pos <= row_pos)
        bias_ref[pl.ds(i * HEAD_DIM, HEAD_DIM), :] = jnp.where(allowed, 0.0, neg_large)
    keys = jnp.concatenate([b[0:rows, :] for b in blocks], axis=0)
    values = jnp.concatenate([b[rows : 2 * rows, :] for b in blocks], axis=0)
    scale = 1.0 / math.sqrt(HEAD_DIM)
    for head in range(HEADS // KV_HEADS):
        lanes = slice(head * HEAD_DIM, (head + 1) * HEAD_DIM)
        scores = dot(q_ref[:, lanes], keys, ((1,), (1,))) * scale + bias_ref[...]
        top = jnp.max(scores, axis=-1, keepdims=True)
        expo = jnp.exp(scores - top)
        weights = (expo * (1.0 / jnp.sum(expo, axis=-1, keepdims=True))).astype(bf16)
        o_ref[:, lanes] = dot(weights, values, ((1,), (0,))).astype(bf16)


def attend(queries, keys, values, segment):
    rows, lanes = keys.shape
    seg_rows = (segment + 1).astype(bf16).reshape(-1, lanes)
    seg_rows = jnp.concatenate([seg_rows, jnp.zeros((14, lanes), bf16)], 0)
    packed = jnp.concatenate([keys, values, seg_rows], 0)
    earlier = [passed_along(packed, "seq", step) for step in (1, 2)]
    vmem = pl.BlockSpec(memory_space=pltpu.VMEM)
    return pl.pallas_call(
        attend_kernel,
        out_shape=jax.ShapeDtypeStruct(queries.shape, bf16),
        in_specs=[vmem] * 4,
        out_specs=vmem,
        scratch_shapes=[pltpu.VMEM((rows, (REACH + 1) * rows), f32)],
        compiler_params=pltpu.CompilerParams(vmem_limit_bytes=24 << 20),
        cost_estimate=pl.CostEstimate(
            flops=4 * rows * 3 * rows * 1024, bytes_accessed=2 << 20, transcendentals=rows * 3 * rows * 8
        ),
        name="attend",
    )(queries, earlier[1], earlier[0], packed)


def dot(a, b, dims):
    return lax.dot_general(a, b, (dims, ((), ())), preferred_element_type=f32)


def hot(a, b):
    return (a == b).astype(bf16)


VMEM = pl.BlockSpec(memory_space=pltpu.VMEM)
SMEM = pl.BlockSpec(memory_space=pltpu.SMEM)


def chunk_of(core, ring, quarter):
    return jnp.where(core == 0, ring * 4 + quarter, quarter * SIDE + ring)


def project_kernel(place_ref, own_ref, other_ref, *refs):
    blocks, out_ref = refs[:SIDE], refs[SIDE]
    core, here = place_ref[0], place_ref[1]
    both = jnp.concatenate([own_ref[...], other_ref[...]], axis=0)
    for distance, block in enumerate(blocks):
        ring = lax.rem(here - distance + SIDE, SIDE)
        y = dot(block[...], both, ((1,), (1,))).astype(bf16)
        for quarter in range(4):
            out_ref[chunk_of(core, ring, quarter)] = y[quarter * 24 : quarter * 24 + 24]


def project(place, own, other, blocks):
    rows, feats = own.shape[0] * 2, own.shape[1]
    return pl.pallas_call(
        project_kernel,
        out_shape=jax.ShapeDtypeStruct((32, 24, rows), bf16),
        in_specs=[SMEM] + [VMEM] * (2 + SIDE),
        out_specs=VMEM,
        compiler_params=pltpu.CompilerParams(vmem_limit_bytes=24 << 20),
        cost_estimate=pl.CostEstimate(
            flops=2 * 768 * rows * feats, bytes_accessed=4 << 20, transcendentals=0
        ),
        name="project",
    )(place, own, other, *blocks)


def term_kernel(place_ref, delta_ref, own_ref, other_ref, out_ref):
    core = place_ref[0]
    both = jnp.concatenate([own_ref[...], other_ref[...]], axis=0)
    for ring in range(SIDE):
        left = jnp.concatenate(
            [delta_ref[chunk_of(core, ring, quarter)] for quarter in range(4)], axis=0
        )
        out_ref[ring] = dot(left, both, ((1,), (0,))).astype(bf16)


def term_of(place, deltas, own, other):
    rows, feats = own.shape[0] * 2, own.shape[1]
    return pl.pallas_call(
        term_kernel,
        out_shape=jax.ShapeDtypeStruct((SIDE, 96, feats), bf16),
        in_specs=[SMEM] + [VMEM] * 3,
        out_specs=VMEM,
        compiler_params=pltpu.CompilerParams(vmem_limit_bytes=24 << 20),
        cost_estimate=pl.CostEstimate(
            flops=2 * 768 * rows * feats, bytes_accessed=4 << 20, transcendentals=0
        ),
        name="term",
    )(place, deltas, own, other)


def spread_of(core):
    block = jnp.arange(192, dtype=i32) // 12
    inner = jnp.arange(192, dtype=i32) % 12
    pair = jnp.where(core == 0, block, (block % 2) * SIDE + block // 2)
    source = 24 * pair + 12 * core + inner
    return hot(jnp.arange(384, dtype=i32)[:, None], source[None, :])


def on_device(queries, keys, values, segment, repack, proj, student_states, target_row):
    rows = queries.shape[0]
    devices = lax.axis_size("seq")
    shares = lax.axis_size("tp")
    share = SW // shares
    index = lax.axis_index("seq")
    core = index % 2
    here = jnp.where(core == 0, index // (2 * SIDE), (index // 2) % SIDE)
    place = jnp.stack([core, here]).astype(i32)
    tp_index = lax.axis_index("tp")
    feats = proj.shape[0]
    near = exchange(to_all(proj, SIDE), NEAR).reshape(SIDE * feats, -1)
    attended = attend(queries, keys, values, segment)
    target_dev = repack // rows
    local_slot = repack - target_dev * rows
    row_ids = jnp.arange(rows, dtype=i32)
    bucket_row = target_dev * GROUP_ROWS + row_ids % GROUP_ROWS
    pick = hot(jnp.arange(devices * GROUP_ROWS, dtype=i32)[:, None], bucket_row[None, :])
    slot_lanes = jnp.broadcast_to(local_slot.astype(bf16)[:, None], (rows, 128))
    attended, near = lax.optimization_barrier((attended, near))
    wide = jnp.concatenate([attended, slot_lanes], 1)
    buckets = dot(pick, wide, ((1,), (0,))).astype(bf16)
    buckets = buckets.reshape(devices, GROUP_ROWS, -1)
    arrived = exchange(buckets).reshape(devices * GROUP_ROWS, -1)
    blocks = [near]
    for distance in range(1, SIDE):
        blocks.append(along_ring(near, distance))
    mine, theirs = spread_of(core), spread_of(1 - core)
    student_part = lax.dynamic_slice_in_dim(student_states, tp_index * share, share, 1)
    chosen = dot(hot(target_row[:, None], row_ids[None, :]), student_part, ((1,), (0,)))
    chosen = chosen.astype(bf16)
    target_own = dot(mine, chosen, ((0,), (1,))).astype(bf16)
    target_other = other_core(dot(theirs, chosen, ((0,), (1,))).astype(bf16))
    target = jnp.concatenate([target_own, target_other], 1)
    arrived, target, blocks = lax.optimization_barrier((arrived, target, blocks))
    slot_hot = hot(arrived[:, 1024:1025].astype(i32), row_ids[None, :])
    own = dot(slot_hot, arrived[:, :1024], ((0,), (0,))).astype(bf16)
    other = other_core(own)
    y_split = project(place, own, other, blocks)
    y_split = y_split.reshape(shares, -1, 2 * rows)
    y_terms = exchange(y_split, axis="tp")
    y_rounded = jnp.sum(y_terms.astype(f32), axis=0).astype(bf16)
    delta = (y_rounded.astype(f32) - target.astype(f32)).astype(bf16)
    deltas = exchange(to_all(delta, shares), axis="tp")
    term = term_of(place, deltas.reshape(32, 24, 2 * rows), own, other)
    far = exchange(term, FAR)
    far = jnp.sum(far.astype(f32), axis=0).astype(bf16)
    last = exchange(far.reshape(SIDE, feats, -1), NEAR)
    norm_factor = 1.0 / math.sqrt(rows * devices)
    grad = jnp.sum(last.astype(f32), axis=0) * norm_factor
    rest = other_core(y_rounded[:, rows:])
    out_rows = dot(y_rounded[:, :rows], mine, ((0,), (1,)))
    out_rows = (out_rows + dot(rest, theirs, ((0,), (1,)))).astype(bf16)
    return (out_rows, grad)


def solution(mesh):
    placed = (
        P("seq", "tp"),
        P("seq", "tp"),
        P("seq", "tp"),
        P("seq"),
        P("seq"),
        P("seq", "tp"),
        P("seq", None),
        P("seq"),
    )
    return jax.shard_map(
        on_device,
        mesh=mesh,
        in_specs=placed,
        out_specs=(P("seq", "tp"), P("seq", "tp")),
        check_vma=False,
    )
```

```python
import math

import jax
import jax.numpy as jnp
from jax import lax
from jax.experimental import pallas as pl
from jax.experimental.pallas import tpu as pltpu
from jax.sharding import PartitionSpec as P


HEADS = 32
KV_HEADS = 4
HEAD_DIM = 128
SW = 1536
REACH = 2
GROUP_ROWS = 4
SIDE = 8

neg_large = -1e30
bf16, f32, i32 = jnp.bfloat16, jnp.float32, jnp.int32


def seq_index(z, y, core):
    return (z * SIDE + y) * 2 + core


NEAR = [[seq_index(z, y, 0) for y in range(SIDE)] for z in range(SIDE)] + [
    [seq_index(z, y, 1) for z in range(SIDE)] for y in range(SIDE)
]
FAR = [[seq_index(z, y, 0) for z in range(SIDE)] for y in range(SIDE)] + [
    [seq_index(z, y, 1) for y in range(SIDE)] for z in range(SIDE)
]


SAME_CORE = [
    [seq_index(z, y, core) for z in range(SIDE) for y in range(SIDE)] for core in range(2)
]


def exchange(block, groups=None, axis="seq"):
    return lax.all_to_all(
        block, axis, split_axis=0, concat_axis=0, tiled=True, axis_index_groups=groups
    )


def passed_along(block, axis, distance):
    devices = range(lax.axis_size(axis))
    route = [(i - distance, i) for i in devices if i - distance in devices]
    return lax.ppermute(block, axis, route)


def along_ring(block, distance):
    route = []
    for z in range(SIDE):
        for y in range(SIDE):
            route.append((seq_index(z, y, 0), seq_index((z + distance) % SIDE, y, 0)))
            route.append((seq_index(z, y, 1), seq_index(z, (y + distance) % SIDE, 1)))
    return lax.ppermute(block, "seq", route)


def other_core(block):
    return lax.ppermute(block, "seq", [(i, i ^ 1) for i in range(lax.axis_size("seq"))])


def to_all(block, count):
    return jnp.broadcast_to(block[None], (count,) + block.shape)


def attend_kernel(q_ref, b2_ref, b1_ref, b0_ref, o_ref, bias_ref):
    rows = q_ref.shape[0]
    blocks = (b2_ref, b1_ref, b0_ref)
    seg_lanes = [
        b[2 * rows + i : 2 * rows + i + 1, :].astype(f32) for b in blocks for i in range(2)
    ]
    seg_keys = jnp.concatenate(seg_lanes, axis=1)
    for i in range(2):
        column = jnp.transpose(jnp.broadcast_to(seg_lanes[4 + i], (HEAD_DIM, HEAD_DIM)))
        column = jnp.concatenate([column] * 6, axis=1)
        row_pos = lax.broadcasted_iota(i32, column.shape, 0) + i * HEAD_DIM
        key_pos = lax.broadcasted_iota(i32, column.shape, 1) - REACH * rows
        allowed = (column == seg_keys) & (key_pos <= row_pos)
        bias_ref[pl.ds(i * HEAD_DIM, HEAD_DIM), :] = jnp.where(allowed, 0.0, neg_large)
    keys = jnp.concatenate([b[0:rows, :] for b in blocks], axis=0)
    values = jnp.concatenate([b[rows : 2 * rows, :] for b in blocks], axis=0)
    scale = 1.0 / math.sqrt(HEAD_DIM)
    for head in range(HEADS // KV_HEADS):
        lanes = slice(head * HEAD_DIM, (head + 1) * HEAD_DIM)
        scores = dot(q_ref[:, lanes], keys, ((1,), (1,))) * scale + bias_ref[...]
        top = jnp.max(scores, axis=-1, keepdims=True)
        expo = jnp.exp(scores - top)
        weights = (expo * (1.0 / jnp.sum(expo, axis=-1, keepdims=True))).astype(bf16)
        o_ref[:, lanes] = dot(weights, values, ((1,), (0,))).astype(bf16)


def attend(queries, keys, values, segment):
    rows, lanes = keys.shape
    seg_rows = (segment + 1).astype(bf16).reshape(-1, lanes)
    seg_rows = jnp.concatenate([seg_rows, jnp.zeros((14, lanes), bf16)], 0)
    packed = jnp.concatenate([keys, values, seg_rows], 0)
    earlier = [passed_along(packed, "seq", step) for step in (1, 2)]
    vmem = pl.BlockSpec(memory_space=pltpu.VMEM)
    return pl.pallas_call(
        attend_kernel,
        out_shape=jax.ShapeDtypeStruct(queries.shape, bf16),
        in_specs=[vmem] * 4,
        out_specs=vmem,
        scratch_shapes=[pltpu.VMEM((rows, (REACH + 1) * rows), f32)],
        compiler_params=pltpu.CompilerParams(vmem_limit_bytes=24 << 20),
        cost_estimate=pl.CostEstimate(
            flops=4 * rows * 3 * rows * 1024, bytes_accessed=2 << 20, transcendentals=rows * 3 * rows * 8
        ),
        name="attend",
    )(queries, earlier[1], earlier[0], packed)


def dot(a, b, dims):
    return lax.dot_general(a, b, (dims, ((), ())), preferred_element_type=f32)


def hot(a, b):
    return (a == b).astype(bf16)


VMEM = pl.BlockSpec(memory_space=pltpu.VMEM)
SMEM = pl.BlockSpec(memory_space=pltpu.SMEM)


def chunk_of(core, ring, quarter):
    return jnp.where(core == 0, ring * 4 + quarter, quarter * SIDE + ring)


def place_kernel(in_ref, out_ref):
    count = out_ref.shape[0]
    arrived = in_ref[...].reshape(count, -1)
    slot = arrived[:, 1024:].astype(f32)
    row = lax.broadcasted_iota(i32, slot.shape, 0)
    owner = lax.rem(row, 2 * GROUP_ROWS) // GROUP_ROWS
    slot = slot + (owner * (count // 2)).astype(f32)
    slot = jnp.concatenate([slot] * (count // 128), axis=1)
    slot_hot = (slot == lax.broadcasted_iota(i32, slot.shape, 1).astype(f32)).astype(bf16)
    out_ref[...] = dot(slot_hot, arrived[:, :1024], ((0,), (0,))).astype(bf16)


def placed_rows(arrived):
    count = arrived.shape[0] * arrived.shape[1]
    return pl.pallas_call(
        place_kernel,
        out_shape=jax.ShapeDtypeStruct((count, 1024), bf16),
        in_specs=[VMEM],
        out_specs=VMEM,
        compiler_params=pltpu.CompilerParams(vmem_limit_bytes=16 << 20),
        cost_estimate=pl.CostEstimate(
            flops=2 * count * count * 1024, bytes_accessed=3 << 20, transcendentals=0
        ),
        name="place",
    )(arrived)


def project_kernel(place_ref, own_ref, other_ref, *refs):
    blocks, out_ref = refs[:SIDE], refs[SIDE]
    core, here = place_ref[0], place_ref[1]
    both = own_ref[...] + other_ref[...]
    for distance, block in enumerate(blocks):
        ring = lax.rem(here - distance + SIDE, SIDE)
        y = dot(block[...], both, ((1,), (1,))).astype(bf16)
        for quarter in range(4):
            out_ref[chunk_of(core, ring, quarter)] = y[quarter * 24 : quarter * 24 + 24]


def project(place, own, other, blocks):
    rows, feats = own.shape
    return pl.pallas_call(
        project_kernel,
        out_shape=jax.ShapeDtypeStruct((32, 24, rows), bf16),
        in_specs=[SMEM] + [VMEM] * (2 + SIDE),
        out_specs=VMEM,
        compiler_params=pltpu.CompilerParams(vmem_limit_bytes=16 << 20),
        cost_estimate=pl.CostEstimate(
            flops=2 * 768 * rows * feats, bytes_accessed=4 << 20, transcendentals=0
        ),
        name="project",
    )(place, own, other, *blocks)


def term_kernel(place_ref, delta_ref, own_ref, other_ref, out_ref):
    core = place_ref[0]
    both = own_ref[...] + other_ref[...]
    for ring in range(SIDE):
        left = jnp.concatenate(
            [delta_ref[chunk_of(core, ring, quarter)] for quarter in range(4)], axis=0
        )
        out_ref[ring] = dot(left, both, ((1,), (0,))).astype(bf16)


def term_of(place, deltas, own, other):
    rows, feats = own.shape
    return pl.pallas_call(
        term_kernel,
        out_shape=jax.ShapeDtypeStruct((SIDE, 96, feats), bf16),
        in_specs=[SMEM] + [VMEM] * 3,
        out_specs=VMEM,
        compiler_params=pltpu.CompilerParams(vmem_limit_bytes=24 << 20),
        cost_estimate=pl.CostEstimate(
            flops=2 * 768 * rows * feats, bytes_accessed=4 << 20, transcendentals=0
        ),
        name="term",
    )(place, deltas, own, other)


def spread_of(core):
    block = jnp.arange(192, dtype=i32) // 12
    inner = jnp.arange(192, dtype=i32) % 12
    pair = jnp.where(core == 0, block, (block % 2) * SIDE + block // 2)
    source = 24 * pair + 12 * core + inner
    return hot(jnp.arange(384, dtype=i32)[:, None], source[None, :])


def on_device(queries, keys, values, segment, repack, proj, student_states, target_row):
    rows = queries.shape[0]
    devices = lax.axis_size("seq")
    shares = lax.axis_size("tp")
    share = SW // shares
    index = lax.axis_index("seq")
    core = index % 2
    here = jnp.where(core == 0, index // (2 * SIDE), (index // 2) % SIDE)
    place = jnp.stack([core, here]).astype(i32)
    tp_index = lax.axis_index("tp")
    feats = proj.shape[0]
    near = exchange(to_all(proj, SIDE), NEAR).reshape(SIDE * feats, -1)
    attended = attend(queries, keys, values, segment)
    target_dev = repack // rows
    local_slot = repack - target_dev * rows
    row_ids = jnp.arange(rows, dtype=i32)
    bucket_row = target_dev * GROUP_ROWS + row_ids % GROUP_ROWS
    pick = hot(jnp.arange(devices * GROUP_ROWS, dtype=i32)[:, None], bucket_row[None, :])
    slot_lanes = jnp.broadcast_to(local_slot.astype(bf16)[:, None], (rows, 128))
    attended, near, place = lax.optimization_barrier((attended, near, place))
    wide = jnp.concatenate([attended, slot_lanes], 1)
    buckets = dot(pick, wide, ((1,), (0,))).astype(bf16)
    buckets = buckets.reshape(devices // 2, 2 * GROUP_ROWS, -1)
    arrived = exchange(buckets, SAME_CORE)
    blocks = [near] * SIDE
    for step in range(1, SIDE // 2 + 1):
        blocks[step] = along_ring(blocks[step - 1], 1)
        if step < SIDE // 2:
            blocks[SIDE - step] = along_ring(blocks[(SIDE - step + 1) % SIDE], -1)
    arrived, blocks = lax.optimization_barrier((arrived, blocks))
    own = placed_rows(arrived)
    other = other_core(own)
    y_split = project(place, own, other, blocks)
    y_split, target_row = lax.optimization_barrier((y_split, target_row))
    mine, theirs = spread_of(core), spread_of(1 - core)
    student_part = lax.dynamic_slice_in_dim(student_states, tp_index * share, share, 1)
    chosen = dot(hot(target_row[:, None], row_ids[None, :]), student_part, ((1,), (0,)))
    chosen = chosen.astype(bf16)
    target_own = dot(mine, chosen, ((0,), (1,))).astype(bf16)
    target_other = other_core(dot(theirs, chosen, ((0,), (1,))).astype(bf16))
    target = jnp.concatenate(
        [
            jnp.where(core == 0, target_own, target_other),
            jnp.where(core == 0, target_other, target_own),
        ],
        1,
    )
    y_split = y_split.reshape(shares, -1, 2 * rows)
    y_terms = exchange(y_split, axis="tp")
    y_rounded = jnp.sum(y_terms.astype(f32), axis=0).astype(bf16)
    delta = (y_rounded.astype(f32) - target.astype(f32)).astype(bf16)
    deltas = exchange(to_all(delta, shares), axis="tp")
    term = term_of(place, deltas.reshape(32, 24, 2 * rows), own, other)
    far = exchange(term, FAR)
    far = jnp.sum(far.astype(f32), axis=0).astype(bf16)
    last = exchange(far.reshape(SIDE, feats, -1), NEAR)
    norm_factor = 1.0 / math.sqrt(rows * devices)
    grad = jnp.sum(last.astype(f32), axis=0) * norm_factor
    first, second = y_rounded[:, :rows], y_rounded[:, rows:]
    rest = other_core(jnp.where(core == 0, second, first))
    out_rows = dot(jnp.where(core == 0, first, second), mine, ((0,), (1,)))
    out_rows = (out_rows + dot(rest, theirs, ((0,), (1,)))).astype(bf16)
    return (out_rows, grad)


def solution(mesh):
    placed = (
        P("seq", "tp"),
        P("seq", "tp"),
        P("seq", "tp"),
        P("seq"),
        P("seq"),
        P("seq", "tp"),
        P("seq", None),
        P("seq"),
    )
    return jax.shard_map(
        on_device,
        mesh=mesh,
        in_specs=placed,
        out_specs=(P("seq", "tp"), P("seq", "tp")),
        check_vma=False,
    )
```

```python
import functools
import math

import jax
import jax.numpy as jnp
from jax import lax
from jax.experimental import pallas as pl
from jax.experimental.pallas import tpu as pltpu
from jax.sharding import PartitionSpec as P


HEADS = 32
KV_HEADS = 4
HEAD_DIM = 128
SW = 1536
REACH = 2
GROUP_ROWS = 4
SIDE = 8

neg_large = -1e30
bf16, f32, i32 = jnp.bfloat16, jnp.float32, jnp.int32


def seq_index(z, y, core):
    return (z * SIDE + y) * 2 + core


NEAR = [[seq_index(z, y, 0) for y in range(SIDE)] for z in range(SIDE)] + [
    [seq_index(z, y, 1) for z in range(SIDE)] for y in range(SIDE)
]
FAR = [[seq_index(z, y, 0) for z in range(SIDE)] for y in range(SIDE)] + [
    [seq_index(z, y, 1) for y in range(SIDE)] for z in range(SIDE)
]


SAME_CORE = [
    [seq_index(z, y, core) for z in range(SIDE) for y in range(SIDE)] for core in range(2)
]


def exchange(block, groups=None, axis="seq"):
    return lax.all_to_all(
        block, axis, split_axis=0, concat_axis=0, tiled=True, axis_index_groups=groups
    )


def passed_along(block, axis, distance):
    devices = range(lax.axis_size(axis))
    route = [(i - distance, i) for i in devices if i - distance in devices]
    return lax.ppermute(block, axis, route)


def other_core(block):
    return lax.ppermute(block, "seq", [(i, i ^ 1) for i in range(lax.axis_size("seq"))])


def to_all(block, count):
    return jnp.broadcast_to(block[None], (count,) + block.shape)


def attend_kernel(q_ref, b2_ref, b1_ref, b0_ref, o_ref, bias_ref):
    rows = q_ref.shape[0]
    blocks = (b2_ref, b1_ref, b0_ref)
    seg_lanes = [
        b[2 * rows + i : 2 * rows + i + 1, :].astype(f32) for b in blocks for i in range(2)
    ]
    seg_keys = jnp.concatenate(seg_lanes, axis=1)
    for i in range(2):
        column = jnp.transpose(jnp.broadcast_to(seg_lanes[4 + i], (HEAD_DIM, HEAD_DIM)))
        column = jnp.concatenate([column] * 6, axis=1)
        row_pos = lax.broadcasted_iota(i32, column.shape, 0) + i * HEAD_DIM
        key_pos = lax.broadcasted_iota(i32, column.shape, 1) - REACH * rows
        allowed = (column == seg_keys) & (key_pos <= row_pos)
        bias_ref[pl.ds(i * HEAD_DIM, HEAD_DIM), :] = jnp.where(allowed, 0.0, neg_large)
    keys = jnp.concatenate([b[0:rows, :] for b in blocks], axis=0)
    values = jnp.concatenate([b[rows : 2 * rows, :] for b in blocks], axis=0)
    scale = 1.0 / math.sqrt(HEAD_DIM)
    for head in range(HEADS // KV_HEADS):
        lanes = slice(head * HEAD_DIM, (head + 1) * HEAD_DIM)
        scores = dot(q_ref[:, lanes], keys, ((1,), (1,))) * scale + bias_ref[...]
        top = jnp.max(scores, axis=-1, keepdims=True)
        expo = jnp.exp(scores - top)
        weights = (expo * (1.0 / jnp.sum(expo, axis=-1, keepdims=True))).astype(bf16)
        o_ref[:, lanes] = dot(weights, values, ((1,), (0,))).astype(bf16)


def attend(queries, keys, values, segment):
    rows, lanes = keys.shape
    seg_rows = (segment + 1).astype(bf16).reshape(-1, lanes)
    seg_rows = jnp.concatenate([seg_rows, jnp.zeros((14, lanes), bf16)], 0)
    packed = jnp.concatenate([keys, values, seg_rows], 0)
    earlier = [passed_along(packed, "seq", step) for step in (1, 2)]
    vmem = pl.BlockSpec(memory_space=pltpu.VMEM)
    return pl.pallas_call(
        attend_kernel,
        out_shape=jax.ShapeDtypeStruct(queries.shape, bf16),
        in_specs=[vmem] * 4,
        out_specs=vmem,
        scratch_shapes=[pltpu.VMEM((rows, (REACH + 1) * rows), f32)],
        compiler_params=pltpu.CompilerParams(vmem_limit_bytes=24 << 20),
        cost_estimate=pl.CostEstimate(
            flops=4 * rows * 3 * rows * 1024, bytes_accessed=2 << 20, transcendentals=rows * 3 * rows * 8
        ),
        name="attend",
    )(queries, earlier[1], earlier[0], packed)


def dot(a, b, dims):
    return lax.dot_general(a, b, (dims, ((), ())), preferred_element_type=f32)


def hot(a, b):
    return (a == b).astype(bf16)


VMEM = pl.BlockSpec(memory_space=pltpu.VMEM)
SMEM = pl.BlockSpec(memory_space=pltpu.SMEM)


def chunk_of(core, ring, quarter):
    return jnp.where(core == 0, ring * 4 + quarter, quarter * SIDE + ring)


def place_kernel(in_ref, out_ref):
    count = out_ref.shape[0]
    arrived = in_ref[...].reshape(count, -1)
    slot = arrived[:, 1024:].astype(f32)
    row = lax.broadcasted_iota(i32, slot.shape, 0)
    owner = lax.rem(row, 2 * GROUP_ROWS) // GROUP_ROWS
    slot = slot + (owner * (count // 2)).astype(f32)
    slot = jnp.concatenate([slot] * (count // 128), axis=1)
    slot_hot = (slot == lax.broadcasted_iota(i32, slot.shape, 1).astype(f32)).astype(bf16)
    out_ref[...] = dot(slot_hot, arrived[:, :1024], ((0,), (0,))).astype(bf16)


def placed_rows(arrived):
    count = arrived.shape[0] * arrived.shape[1]
    return pl.pallas_call(
        place_kernel,
        out_shape=jax.ShapeDtypeStruct((count, 1024), bf16),
        in_specs=[VMEM],
        out_specs=VMEM,
        compiler_params=pltpu.CompilerParams(vmem_limit_bytes=16 << 20),
        cost_estimate=pl.CostEstimate(
            flops=2 * count * count * 1024, bytes_accessed=3 << 20, transcendentals=0
        ),
        name="place",
    )(arrived)


def project_kernel(add, place_ref, own_ref, other_ref, proj_ref, out_ref):
    core, share = place_ref[0], place_ref[1]
    if add:
        both = own_ref[...] + other_ref[...]
    else:
        both = jnp.concatenate([own_ref[...], other_ref[...]], axis=0)
    for ring in range(SIDE):
        y = dot(proj_ref[ring * 96 : ring * 96 + 96], both, ((1,), (1,))).astype(bf16)
        for quarter in range(4):
            chunk = chunk_of(core, ring, quarter)
            away = lax.rem(chunk // 8 - share + 4, 4)
            out_ref[away, lax.rem(chunk, 8)] = y[quarter * 24 : quarter * 24 + 24]


def project(place, own, other, half_proj, add):
    feats = own.shape[1]
    rows = own.shape[0] if add else 2 * own.shape[0]
    return pl.pallas_call(
        functools.partial(project_kernel, add),
        out_shape=jax.ShapeDtypeStruct((4, 8, 24, rows), bf16),
        in_specs=[SMEM] + [VMEM] * 3,
        out_specs=VMEM,
        compiler_params=pltpu.CompilerParams(vmem_limit_bytes=16 << 20),
        cost_estimate=pl.CostEstimate(
            flops=2 * 768 * rows * feats, bytes_accessed=4 << 20, transcendentals=0
        ),
    )(place, own, other, half_proj)


def term_kernel(place_ref, *refs):
    parts, (target_ref, own_ref, other_ref, own_m_ref, other_m_ref, out_ref, held) = refs[:4], refs[4:]
    core, share = place_ref[0], place_ref[1]
    for i, part in enumerate(parts):
        held[i] = part[...]
    attended = jnp.concatenate([own_ref[...], other_ref[...]], axis=0)
    moved = own_m_ref[...] + other_m_ref[...]
    for ring in range(SIDE):
        left, right = [], []
        for quarter in range(4):
            chunk = chunk_of(core, ring, quarter)
            away = lax.rem(share - chunk // 8 + 4, 4)
            left.append(held[away, lax.rem(chunk, 8)])
            right.append(target_ref[chunk])
        y_part = dot(jnp.concatenate(left, axis=0), attended, ((1,), (0,)))
        t_part = dot(jnp.concatenate(right, axis=0), moved, ((1,), (0,)))
        out_ref[ring] = (y_part - t_part).astype(bf16)


def term_of(place, parts, targets, own, other, own_m, other_m):
    rows, feats = own_m.shape
    return pl.pallas_call(
        term_kernel,
        out_shape=jax.ShapeDtypeStruct((SIDE, 96, feats), bf16),
        in_specs=[SMEM] + [VMEM] * 9,
        out_specs=VMEM,
        scratch_shapes=[pltpu.VMEM((4, 8, 24, rows), bf16)],
        compiler_params=pltpu.CompilerParams(vmem_limit_bytes=24 << 20),
        cost_estimate=pl.CostEstimate(
            flops=4 * 768 * rows * feats, bytes_accessed=8 << 20, transcendentals=0
        ),
        name="term",
    )(place, *parts, targets, own, other, own_m, other_m)


def share_route(distance):
    return [(i, (i + distance) % 4) for i in range(4)]


def summed_share(y_split):
    total = y_split[0].astype(f32)
    got = [lax.ppermute(y_split[k], "tp", share_route(k)) for k in range(1, 4)]
    for part in got:
        total = total + part.astype(f32)
    return total.astype(bf16)


def spread_of(core):
    block = jnp.arange(192, dtype=i32) // 12
    inner = jnp.arange(192, dtype=i32) % 12
    pair = jnp.where(core == 0, block, (block % 2) * SIDE + block // 2)
    source = 24 * pair + 12 * core + inner
    return hot(jnp.arange(384, dtype=i32)[:, None], source[None, :])


def on_device(queries, keys, values, segment, repack, proj, student_states, target_row):
    rows = queries.shape[0]
    devices = lax.axis_size("seq")
    shares = lax.axis_size("tp")
    share = SW // shares
    core = lax.axis_index("seq") % 2
    tp_index = lax.axis_index("tp")
    place = jnp.stack([core, tp_index]).astype(i32)
    feats = proj.shape[0]
    row_ids = jnp.arange(rows, dtype=i32)
    near = exchange(to_all(proj, SIDE), NEAR).reshape(SIDE * feats, -1)
    queries, near, place = lax.optimization_barrier((queries, near, place))
    half_proj = exchange(to_all(near, SIDE), FAR).reshape(SIDE * SIDE * feats, -1)
    attended = attend(queries, keys, values, segment)
    partner = other_core(attended)
    target_dev = repack // rows
    local_slot = repack - target_dev * rows
    bucket_row = target_dev * GROUP_ROWS + row_ids % GROUP_ROWS
    pick = hot(jnp.arange(devices * GROUP_ROWS, dtype=i32)[:, None], bucket_row[None, :])
    slot_lanes = jnp.broadcast_to(local_slot.astype(bf16)[:, None], (rows, 128))
    wide = jnp.concatenate([attended, slot_lanes], 1)
    buckets = dot(pick, wide, ((1,), (0,))).astype(bf16)
    buckets = buckets.reshape(devices // 2, 2 * GROUP_ROWS, -1)
    mine, theirs = spread_of(core), spread_of(1 - core)
    chosen = dot(hot(target_row[:, None], row_ids[None, :]), student_states, ((1,), (0,)))
    chosen = chosen.astype(bf16)
    chosen = [chosen[:, i * share : (i + 1) * share] for i in range(shares)]
    target_own = jnp.concatenate([dot(mine, c, ((0,), (1,))) for c in chosen], 0).astype(bf16)
    target_other = jnp.concatenate([dot(theirs, c, ((0,), (1,))) for c in chosen], 0)
    target_other = other_core(target_other.astype(bf16))
    targets = jnp.concatenate(
        [
            jnp.where(core == 0, target_own, target_other),
            jnp.where(core == 0, target_other, target_own),
        ],
        1,
    )
    buckets, half_proj, targets = lax.optimization_barrier((buckets, half_proj, targets))
    arrived = exchange(buckets, SAME_CORE)
    y_split = project(place, attended, partner, half_proj, False)
    y_teacher = summed_share(y_split)
    parts = [y_teacher]
    for distance in range(1, shares):
        parts.append(lax.ppermute(y_teacher, "tp", share_route(distance)))
    arrived, parts[1] = lax.optimization_barrier((arrived, parts[1]))
    own = placed_rows(arrived)
    other = other_core(own)
    term = term_of(place, parts, targets.reshape(32, 24, 2 * rows), attended, partner, own, other)
    term, own = lax.optimization_barrier((term, own))
    far = exchange(term, FAR)
    far = jnp.sum(far.astype(f32), axis=0).astype(bf16)
    last = exchange(far.reshape(SIDE, feats, -1), NEAR)
    norm_factor = 1.0 / math.sqrt(rows * devices)
    grad = jnp.sum(last.astype(f32), axis=0) * norm_factor
    y_split = project(place, own, other, half_proj, True)
    y_rows = summed_share(y_split).reshape(-1, 2 * rows)
    first, second = y_rows[:, :rows], y_rows[:, rows:]
    rest = other_core(jnp.where(core == 0, second, first))
    out_rows = dot(jnp.where(core == 0, first, second), mine, ((0,), (1,)))
    out_rows = (out_rows + dot(rest, theirs, ((0,), (1,)))).astype(bf16)
    return (out_rows, grad)


def solution(mesh):
    placed = (
        P("seq", "tp"),
        P("seq", "tp"),
        P("seq", "tp"),
        P("seq"),
        P("seq"),
        P("seq", "tp"),
        P("seq", None),
        P("seq"),
    )
    return jax.shard_map(
        on_device,
        mesh=mesh,
        in_specs=placed,
        out_specs=(P("seq", "tp"), P("seq", "tp")),
        check_vma=False,
    )
```

```python
import functools
import math

import jax
import jax.numpy as jnp
from jax import lax
from jax.experimental import pallas as pl
from jax.experimental.pallas import tpu as pltpu
from jax.sharding import PartitionSpec as P


HEADS = 32
KV_HEADS = 4
HEAD_DIM = 128
REACH = 2
GROUP_ROWS = 4
SIDE = 8

VMEM = pl.BlockSpec(memory_space=pltpu.VMEM)
SMEM = pl.BlockSpec(memory_space=pltpu.SMEM)

neg_large = -1e30
bf16, f32, i32 = jnp.bfloat16, jnp.float32, jnp.int32


def seq_index(z, y, core):
    return (z * SIDE + y) * 2 + core


NEAR = [[seq_index(z, y, 0) for y in range(SIDE)] for z in range(SIDE)] + [
    [seq_index(z, y, 1) for z in range(SIDE)] for y in range(SIDE)
]
FAR = [[seq_index(z, y, 0) for z in range(SIDE)] for y in range(SIDE)] + [
    [seq_index(z, y, 1) for y in range(SIDE)] for z in range(SIDE)
]


SAME_CORE = [
    [seq_index(z, y, core) for z in range(SIDE) for y in range(SIDE)] for core in range(2)
]


def exchange(block, groups=None, axis="seq"):
    return lax.all_to_all(
        block, axis, split_axis=0, concat_axis=0, tiled=True, axis_index_groups=groups
    )


def passed_along(block, axis, distance):
    devices = range(lax.axis_size(axis))
    route = [(i - distance, i) for i in devices if i - distance in devices]
    return lax.ppermute(block, axis, route)


def other_core(block):
    return lax.ppermute(block, "seq", [(i, i ^ 1) for i in range(lax.axis_size("seq"))])


def to_all(block, count):
    return jnp.broadcast_to(block[None], (count,) + block.shape)


def attend_kernel(q_any, b2_ref, b1_ref, b0_ref, o_ref, bias_ref, q_ref, sem):
    load = pltpu.make_async_copy(q_any, q_ref, sem)
    load.start()
    rows = q_ref.shape[0]
    blocks = (b2_ref, b1_ref, b0_ref)
    seg_lanes = [
        b[2 * rows + i : 2 * rows + i + 1, :].astype(f32) for b in blocks for i in range(2)
    ]
    seg_keys = jnp.concatenate(seg_lanes, axis=1)
    for i in range(2):
        column = jnp.transpose(jnp.broadcast_to(seg_lanes[4 + i], (HEAD_DIM, HEAD_DIM)))
        column = jnp.concatenate([column] * 6, axis=1)
        row_pos = lax.broadcasted_iota(i32, column.shape, 0) + i * HEAD_DIM
        key_pos = lax.broadcasted_iota(i32, column.shape, 1) - REACH * rows
        allowed = (column == seg_keys) & (key_pos <= row_pos)
        bias_ref[pl.ds(i * HEAD_DIM, HEAD_DIM), :] = jnp.where(allowed, 0.0, neg_large)
    keys = jnp.concatenate([b[0:rows, :] for b in blocks], axis=0)
    values = jnp.concatenate([b[rows : 2 * rows, :] for b in blocks], axis=0)
    scale = 1.0 / math.sqrt(HEAD_DIM)
    load.wait()
    for head in range(HEADS // KV_HEADS):
        lanes = slice(head * HEAD_DIM, (head + 1) * HEAD_DIM)
        scores = dot(q_ref[:, lanes], keys, ((1,), (1,))) * scale + bias_ref[...]
        top = jnp.max(scores, axis=-1, keepdims=True)
        expo = jnp.exp(scores - top)
        weights = (expo * (1.0 / jnp.sum(expo, axis=-1, keepdims=True))).astype(bf16)
        o_ref[:, lanes] = dot(weights, values, ((1,), (0,))).astype(bf16)


def packed_rows(keys, values, segment):
    lanes = keys.shape[1]
    seg_rows = (segment + 1).astype(bf16).reshape(-1, lanes)
    seg_rows = jnp.concatenate([seg_rows, jnp.zeros((14, lanes), bf16)], 0)
    return jnp.concatenate([keys, values, seg_rows], 0)


def attend(queries, two_before, one_before, packed):
    rows = queries.shape[0]
    return pl.pallas_call(
        attend_kernel,
        out_shape=jax.ShapeDtypeStruct(queries.shape, bf16),
        in_specs=[pl.BlockSpec(memory_space=pl.ANY)] + [VMEM] * 3,
        out_specs=VMEM,
        scratch_shapes=[
            pltpu.VMEM((rows, (REACH + 1) * rows), f32),
            pltpu.VMEM(queries.shape, bf16),
            pltpu.SemaphoreType.DMA,
        ],
        compiler_params=pltpu.CompilerParams(vmem_limit_bytes=24 << 20),
        cost_estimate=pl.CostEstimate(
            flops=4 * rows * 3 * rows * 1024, bytes_accessed=2 << 20, transcendentals=rows * 3 * rows * 8
        ),
        name="attend",
    )(queries, two_before, one_before, packed)


def dot(a, b, dims):
    return lax.dot_general(a, b, (dims, ((), ())), preferred_element_type=f32)


def hot(a, b):
    return (a == b).astype(bf16)


def chunk_of(core, ring, quarter):
    return jnp.where(core == 0, ring * 4 + quarter, quarter * SIDE + ring)


def place_kernel(in_ref, out_ref):
    count = out_ref.shape[0]
    arrived = in_ref[...].reshape(count, -1)
    slot = arrived[:, 1024:].astype(f32)
    row = lax.broadcasted_iota(i32, slot.shape, 0)
    owner = lax.rem(row, 2 * GROUP_ROWS) // GROUP_ROWS
    slot = slot + (owner * (count // 2)).astype(f32)
    slot = jnp.concatenate([slot] * (count // 128), axis=1)
    slot_hot = (slot == lax.broadcasted_iota(i32, slot.shape, 1).astype(f32)).astype(bf16)
    out_ref[...] = dot(slot_hot, arrived[:, :1024], ((0,), (0,))).astype(bf16)


def placed_rows(arrived):
    count = arrived.shape[0] * arrived.shape[1]
    return pl.pallas_call(
        place_kernel,
        out_shape=jax.ShapeDtypeStruct((count, 1024), bf16),
        in_specs=[VMEM],
        out_specs=VMEM,
        compiler_params=pltpu.CompilerParams(vmem_limit_bytes=16 << 20),
        cost_estimate=pl.CostEstimate(
            flops=2 * count * count * 1024, bytes_accessed=3 << 20, transcendentals=0
        ),
        name="place",
    )(arrived)


def project_kernel(add, place_ref, own_ref, other_ref, proj_ref, out_ref):
    core, share = place_ref[0], place_ref[1]
    if add:
        both = own_ref[...] + other_ref[...]
    else:
        both = jnp.concatenate([own_ref[...], other_ref[...]], axis=0)
    for ring in range(SIDE):
        y = dot(proj_ref[ring * 96 : ring * 96 + 96], both, ((1,), (1,))).astype(bf16)
        for quarter in range(4):
            chunk = chunk_of(core, ring, quarter)
            away = lax.rem(chunk // 8 - share + 4, 4)
            out_ref[away, lax.rem(chunk, 8)] = y[quarter * 24 : quarter * 24 + 24]


def project(place, own, other, half_proj, add):
    feats = own.shape[1]
    rows = own.shape[0] if add else 2 * own.shape[0]
    return pl.pallas_call(
        functools.partial(project_kernel, add),
        out_shape=jax.ShapeDtypeStruct((4, 8, 24, rows), bf16),
        in_specs=[SMEM] + [VMEM] * 3,
        out_specs=VMEM,
        compiler_params=pltpu.CompilerParams(vmem_limit_bytes=16 << 20),
        cost_estimate=pl.CostEstimate(
            flops=2 * 768 * rows * feats, bytes_accessed=4 << 20, transcendentals=0
        ),
    )(place, own, other, half_proj)


def targets_kernel(row_ref, states_ref, mine_ref, theirs_ref, own_ref, other_ref):
    rows = states_ref.shape[0]
    source = lax.broadcasted_iota(i32, (rows, rows), 0)
    chosen = jnp.where(source == row_ref[...], 1.0, 0.0).astype(bf16)
    for spread_ref, out_ref in ((mine_ref, own_ref), (theirs_ref, other_ref)):
        for share in range(4):
            states = states_ref[:, share * 384 : share * 384 + 384]
            part = dot(spread_ref[...], states, ((0,), (1,))).astype(bf16)
            part = dot(part, chosen, ((1,), (0,))).astype(bf16)
            for quarter in range(8):
                out_ref[share * 8 + quarter] = part[quarter * 24 : quarter * 24 + 24]


def targets_of(target_row, student_states, mine, theirs):
    rows = student_states.shape[0]
    out = jax.ShapeDtypeStruct((32, 24, rows), bf16)
    return pl.pallas_call(
        targets_kernel,
        out_shape=(out, out),
        in_specs=[VMEM] * 4,
        out_specs=(VMEM, VMEM),
        compiler_params=pltpu.CompilerParams(vmem_limit_bytes=16 << 20),
        cost_estimate=pl.CostEstimate(
            flops=2 * 1536 * rows * (384 + 256), bytes_accessed=2 << 20, transcendentals=0
        ),
        name="targets",
    )(target_row.reshape(1, rows), student_states, mine, theirs)


def term_kernel(place_ref, *refs):
    parts, refs = refs[:4], refs[4:]
    own_t, other_t, own_ref, other_ref, own_m, other_m, out_ref, held, moved = refs
    core, share = place_ref[0], place_ref[1]
    half = own_t.shape[2]
    for i, part in enumerate(parts):
        held[i] = part[...]
    attended = jnp.concatenate([own_ref[...], other_ref[...]], axis=0)
    moved[...] = own_m[...] + other_m[...]
    right = [moved[pl.ds(c * half, half), :] for c in (core, 1 - core)]
    for ring in range(SIDE):
        chunks = [chunk_of(core, ring, quarter) for quarter in range(4)]
        left = [held[lax.rem(share - k // 8 + 4, 4), lax.rem(k, 8)] for k in chunks]
        total = dot(jnp.concatenate(left, axis=0), attended, ((1,), (0,)))
        for target_ref, rows in zip((own_t, other_t), right):
            left = jnp.concatenate([target_ref[k] for k in chunks], axis=0)
            total = total - dot(left, rows, ((1,), (0,)))
        out_ref[ring] = total.astype(bf16)


def term_of(place, parts, targets, own, other, own_m, other_m):
    rows, feats = own_m.shape
    return pl.pallas_call(
        term_kernel,
        out_shape=jax.ShapeDtypeStruct((SIDE, 96, feats), bf16),
        in_specs=[SMEM] + [VMEM] * 10,
        out_specs=VMEM,
        scratch_shapes=[pltpu.VMEM((4, 8, 24, rows), bf16), pltpu.VMEM((rows, feats), bf16)],
        compiler_params=pltpu.CompilerParams(vmem_limit_bytes=24 << 20),
        cost_estimate=pl.CostEstimate(
            flops=4 * 768 * rows * feats, bytes_accessed=8 << 20, transcendentals=0
        ),
        name="term",
    )(place, *parts, *targets, own, other, own_m, other_m)


def share_route(distance):
    return [(i, (i + distance) % 4) for i in range(4)]


def summed_share(y_split):
    total = y_split[0].astype(f32)
    got = [lax.ppermute(y_split[k], "tp", share_route(k)) for k in range(1, 4)]
    for part in got:
        total = total + part.astype(f32)
    return total.astype(bf16)


def spread_of(core):
    block = jnp.arange(192, dtype=i32) // 12
    inner = jnp.arange(192, dtype=i32) % 12
    pair = jnp.where(core == 0, block, (block % 2) * SIDE + block // 2)
    source = 24 * pair + 12 * core + inner
    return hot(jnp.arange(384, dtype=i32)[:, None], source[None, :])


def on_device(queries, keys, values, segment, repack, proj, student_states, target_row):
    rows = queries.shape[0]
    devices = lax.axis_size("seq")
    shares = lax.axis_size("tp")
    core = lax.axis_index("seq") % 2
    tp_index = lax.axis_index("tp")
    place = jnp.stack([core, tp_index]).astype(i32)
    feats = proj.shape[0]
    row_ids = jnp.arange(rows, dtype=i32)
    near = exchange(to_all(proj, SIDE), NEAR).reshape(SIDE * feats, -1)
    packed = packed_rows(keys, values, segment)
    one_before = passed_along(packed, "seq", 1)
    two_before = passed_along(packed, "seq", 2)
    queries, near, place = lax.optimization_barrier((queries, near, place))
    half_proj = exchange(to_all(near, SIDE), FAR).reshape(SIDE * SIDE * feats, -1)
    attended = attend(queries, two_before, one_before, packed)
    partner = other_core(attended)
    target_dev = repack // rows
    local_slot = repack - target_dev * rows
    bucket_row = target_dev * GROUP_ROWS + row_ids % GROUP_ROWS
    pick = hot(jnp.arange(devices * GROUP_ROWS, dtype=i32)[:, None], bucket_row[None, :])
    slot_lanes = jnp.broadcast_to(local_slot.astype(bf16)[:, None], (rows, 128))
    wide = jnp.concatenate([attended, slot_lanes], 1)
    buckets = dot(pick, wide, ((1,), (0,))).astype(bf16)
    buckets = buckets.reshape(devices // 2, 2 * GROUP_ROWS, -1)
    buckets, half_proj = lax.optimization_barrier((buckets, half_proj))
    arrived = exchange(buckets, SAME_CORE)
    y_split = project(place, attended, partner, half_proj, False)
    y_split, target_row = lax.optimization_barrier((y_split, target_row))
    mine, theirs = spread_of(core), spread_of(1 - core)
    target_own, target_other = targets_of(target_row, student_states, mine, theirs)
    target_other = other_core(target_other)
    y_teacher = summed_share(y_split)
    parts = [y_teacher]
    for distance in range(1, shares):
        parts.append(lax.ppermute(y_teacher, "tp", share_route(distance)))
    arrived, parts[1] = lax.optimization_barrier((arrived, parts[1]))
    own = placed_rows(arrived)
    other = other_core(own)
    targets = (target_own, target_other)
    term = term_of(place, parts, targets, attended, partner, own, other)
    far = exchange(term, FAR)
    far = jnp.sum(far.astype(f32), axis=0).astype(bf16)
    last = exchange(far.reshape(SIDE, feats, -1), NEAR)
    norm_factor = 1.0 / math.sqrt(rows * devices)
    grad = jnp.sum(last.astype(f32), axis=0) * norm_factor
    y_split = project(place, own, other, half_proj, True)
    y_rows = summed_share(y_split).reshape(-1, 2 * rows)
    first, second = y_rows[:, :rows], y_rows[:, rows:]
    rest = other_core(jnp.where(core == 0, second, first))
    out_rows = dot(jnp.where(core == 0, first, second), mine, ((0,), (1,)))
    out_rows = (out_rows + dot(rest, theirs, ((0,), (1,)))).astype(bf16)
    return (out_rows, grad)


def solution(mesh):
    placed = (
        P("seq", "tp"),
        P("seq", "tp"),
        P("seq", "tp"),
        P("seq"),
        P("seq"),
        P("seq", "tp"),
        P("seq", None),
        P("seq"),
    )
    return jax.shard_map(
        on_device,
        mesh=mesh,
        in_specs=placed,
        out_specs=(P("seq", "tp"), P("seq", "tp")),
        check_vma=False,
    )
```

```python
import functools
import math

import jax
import jax.numpy as jnp
from jax import lax
from jax.experimental import pallas as pl
from jax.experimental.pallas import tpu as pltpu
from jax.sharding import PartitionSpec as P


HEADS = 32
KV_HEADS = 4
HEAD_DIM = 128
REACH = 2
GROUP_ROWS = 4
SIDE = 8

VMEM = pl.BlockSpec(memory_space=pltpu.VMEM)
SMEM = pl.BlockSpec(memory_space=pltpu.SMEM)

neg_large = -1e30
bf16, f32, i32 = jnp.bfloat16, jnp.float32, jnp.int32


def seq_index(z, y, core):
    return (z * SIDE + y) * 2 + core


NEAR = [[seq_index(z, y, 0) for y in range(SIDE)] for z in range(SIDE)] + [
    [seq_index(z, y, 1) for z in range(SIDE)] for y in range(SIDE)
]
FAR = [[seq_index(z, y, 0) for z in range(SIDE)] for y in range(SIDE)] + [
    [seq_index(z, y, 1) for y in range(SIDE)] for z in range(SIDE)
]


SAME_CORE = [
    [seq_index(z, y, core) for z in range(SIDE) for y in range(SIDE)] for core in range(2)
]


def exchange(block, groups=None, axis="seq"):
    return lax.all_to_all(
        block, axis, split_axis=0, concat_axis=0, tiled=True, axis_index_groups=groups
    )


def passed_along(block, axis, distance):
    devices = range(lax.axis_size(axis))
    route = [(i - distance, i) for i in devices if i - distance in devices]
    return lax.ppermute(block, axis, route)


def other_core(block):
    return lax.ppermute(block, "seq", [(i, i ^ 1) for i in range(lax.axis_size("seq"))])


def to_all(block, count):
    return jnp.broadcast_to(block[None], (count,) + block.shape)


def attend_kernel(q_any, b2_ref, b1_ref, b0_ref, o_ref, bias_ref, q_ref, sem):
    load = pltpu.make_async_copy(q_any, q_ref, sem)
    load.start()
    rows = q_ref.shape[0]
    blocks = (b2_ref, b1_ref, b0_ref)
    seg_lanes = [
        b[2 * rows + i : 2 * rows + i + 1, :].astype(f32) for b in blocks for i in range(2)
    ]
    seg_keys = jnp.concatenate(seg_lanes, axis=1)
    for i in range(2):
        column = jnp.transpose(jnp.broadcast_to(seg_lanes[4 + i], (HEAD_DIM, HEAD_DIM)))
        column = jnp.concatenate([column] * 6, axis=1)
        row_pos = lax.broadcasted_iota(i32, column.shape, 0) + i * HEAD_DIM
        key_pos = lax.broadcasted_iota(i32, column.shape, 1) - REACH * rows
        allowed = (column == seg_keys) & (key_pos <= row_pos)
        bias_ref[pl.ds(i * HEAD_DIM, HEAD_DIM), :] = jnp.where(allowed, 0.0, neg_large)
    keys = jnp.concatenate([b[0:rows, :] for b in blocks], axis=0)
    values = jnp.concatenate([b[rows : 2 * rows, :] for b in blocks], axis=0)
    scale = 1.0 / math.sqrt(HEAD_DIM)
    load.wait()
    for head in range(HEADS // KV_HEADS):
        lanes = slice(head * HEAD_DIM, (head + 1) * HEAD_DIM)
        scores = dot(q_ref[:, lanes], keys, ((1,), (1,))) * scale + bias_ref[...]
        top = jnp.max(scores, axis=-1, keepdims=True)
        expo = jnp.exp(scores - top)
        weights = (expo * (1.0 / jnp.sum(expo, axis=-1, keepdims=True))).astype(bf16)
        o_ref[:, lanes] = dot(weights, values, ((1,), (0,))).astype(bf16)


def packed_rows(keys, values, segment):
    lanes = keys.shape[1]
    seg_rows = (segment + 1).astype(bf16).reshape(-1, lanes)
    seg_rows = jnp.concatenate([seg_rows, jnp.zeros((14, lanes), bf16)], 0)
    return jnp.concatenate([keys, values, seg_rows], 0)


def attend(queries, two_before, one_before, packed):
    rows = queries.shape[0]
    return pl.pallas_call(
        attend_kernel,
        out_shape=jax.ShapeDtypeStruct(queries.shape, bf16),
        in_specs=[pl.BlockSpec(memory_space=pl.ANY)] + [VMEM] * 3,
        out_specs=VMEM,
        scratch_shapes=[
            pltpu.VMEM((rows, (REACH + 1) * rows), f32),
            pltpu.VMEM(queries.shape, bf16),
            pltpu.SemaphoreType.DMA,
        ],
        compiler_params=pltpu.CompilerParams(vmem_limit_bytes=24 << 20),
        cost_estimate=pl.CostEstimate(
            flops=4 * rows * 3 * rows * 1024, bytes_accessed=2 << 20, transcendentals=rows * 3 * rows * 8
        ),
        name="attend",
    )(queries, two_before, one_before, packed)


def dot(a, b, dims):
    return lax.dot_general(a, b, (dims, ((), ())), preferred_element_type=f32)


def hot(a, b):
    return (a == b).astype(bf16)


def chunk_of(core, ring, quarter):
    return jnp.where(core == 0, ring * 4 + quarter, quarter * SIDE + ring)


def place_kernel(in_ref, out_ref):
    count = out_ref.shape[0]
    arrived = in_ref[...].reshape(count, -1)
    slot = arrived[:, 1024:].astype(f32)
    row = lax.broadcasted_iota(i32, slot.shape, 0)
    owner = lax.rem(row, 2 * GROUP_ROWS) // GROUP_ROWS
    slot = slot + (owner * (count // 2)).astype(f32)
    slot = jnp.concatenate([slot] * (count // 128), axis=1)
    slot_hot = (slot == lax.broadcasted_iota(i32, slot.shape, 1).astype(f32)).astype(bf16)
    out_ref[...] = dot(slot_hot, arrived[:, :1024], ((0,), (0,))).astype(bf16)


def placed_rows(arrived):
    count = arrived.shape[0] * arrived.shape[1]
    return pl.pallas_call(
        place_kernel,
        out_shape=jax.ShapeDtypeStruct((count, 1024), bf16),
        in_specs=[VMEM],
        out_specs=VMEM,
        compiler_params=pltpu.CompilerParams(vmem_limit_bytes=16 << 20),
        cost_estimate=pl.CostEstimate(
            flops=2 * count * count * 1024, bytes_accessed=3 << 20, transcendentals=0
        ),
        name="place",
    )(arrived)


def project_kernel(add, place_ref, own_ref, other_ref, proj_ref, out_ref):
    core, share = place_ref[0], place_ref[1]
    if add:
        both = own_ref[...] + other_ref[...]
    else:
        both = jnp.concatenate([own_ref[...], other_ref[...]], axis=0)
    for ring in range(SIDE):
        y = dot(proj_ref[ring * 96 : ring * 96 + 96], both, ((1,), (1,))).astype(bf16)
        for quarter in range(4):
            chunk = chunk_of(core, ring, quarter)
            away = lax.rem(chunk // 8 - share + 4, 4)
            out_ref[away, lax.rem(chunk, 8)] = y[quarter * 24 : quarter * 24 + 24]


def project(place, own, other, half_proj, add):
    feats = own.shape[1]
    rows = own.shape[0] if add else 2 * own.shape[0]
    return pl.pallas_call(
        functools.partial(project_kernel, add),
        out_shape=jax.ShapeDtypeStruct((4, 8, 24, rows), bf16),
        in_specs=[SMEM] + [VMEM] * 3,
        out_specs=VMEM,
        compiler_params=pltpu.CompilerParams(vmem_limit_bytes=16 << 20),
        cost_estimate=pl.CostEstimate(
            flops=2 * 768 * rows * feats, bytes_accessed=4 << 20, transcendentals=0
        ),
    )(place, own, other, half_proj)


def targets_kernel(row_ref, states_ref, mine_ref, theirs_ref, own_ref, other_ref):
    rows = states_ref.shape[0]
    source = lax.broadcasted_iota(i32, (rows, rows), 0)
    chosen = jnp.where(source == row_ref[...], 1.0, 0.0).astype(bf16)
    for spread_ref, out_ref in ((mine_ref, own_ref), (theirs_ref, other_ref)):
        for share in range(4):
            states = states_ref[:, share * 384 : share * 384 + 384]
            part = dot(spread_ref[...], states, ((0,), (1,))).astype(bf16)
            part = dot(part, chosen, ((1,), (0,))).astype(bf16)
            for quarter in range(8):
                out_ref[share * 8 + quarter] = part[quarter * 24 : quarter * 24 + 24]


def targets_of(target_row, student_states, mine, theirs):
    rows = student_states.shape[0]
    out = jax.ShapeDtypeStruct((32, 24, rows), bf16)
    return pl.pallas_call(
        targets_kernel,
        out_shape=(out, out),
        in_specs=[VMEM] * 4,
        out_specs=(VMEM, VMEM),
        compiler_params=pltpu.CompilerParams(vmem_limit_bytes=16 << 20),
        cost_estimate=pl.CostEstimate(
            flops=2 * 1536 * rows * (384 + 256), bytes_accessed=2 << 20, transcendentals=0
        ),
        name="targets",
    )(target_row.reshape(1, rows), student_states, mine, theirs)


def term_kernel(place_ref, *refs):
    parts, refs = refs[:4], refs[4:]
    own_t, other_t, own_ref, other_ref, own_m, other_m, out_ref, held, moved = refs
    core, share = place_ref[0], place_ref[1]
    half = own_t.shape[2]
    for i, part in enumerate(parts):
        held[i] = part[...]
    attended = jnp.concatenate([own_ref[...], other_ref[...]], axis=0)
    moved[...] = own_m[...] + other_m[...]
    right = [moved[pl.ds(c * half, half), :] for c in (core, 1 - core)]
    for ring in range(SIDE):
        chunks = [chunk_of(core, ring, quarter) for quarter in range(4)]
        left = [held[lax.rem(share - k // 8 + 4, 4), lax.rem(k, 8)] for k in chunks]
        total = dot(jnp.concatenate(left, axis=0), attended, ((1,), (0,)))
        for target_ref, rows in zip((own_t, other_t), right):
            left = jnp.concatenate([target_ref[k] for k in chunks], axis=0)
            total = total - dot(left, rows, ((1,), (0,)))
        out_ref[ring] = total.astype(bf16)


def term_of(place, parts, targets, own, other, own_m, other_m):
    rows, feats = own_m.shape
    return pl.pallas_call(
        term_kernel,
        out_shape=jax.ShapeDtypeStruct((SIDE, 96, feats), bf16),
        in_specs=[SMEM] + [VMEM] * 10,
        out_specs=VMEM,
        scratch_shapes=[pltpu.VMEM((4, 8, 24, rows), bf16), pltpu.VMEM((rows, feats), bf16)],
        compiler_params=pltpu.CompilerParams(vmem_limit_bytes=24 << 20),
        cost_estimate=pl.CostEstimate(
            flops=4 * 768 * rows * feats, bytes_accessed=8 << 20, transcendentals=0
        ),
        name="term",
    )(place, *parts, *targets, own, other, own_m, other_m)


def share_route(distance):
    return [(i, (i + distance) % 4) for i in range(4)]


def summed_share(y_split, after=None):
    total = y_split[0].astype(f32)
    got = [lax.ppermute(y_split[k], "tp", share_route(k)) for k in range(1, 4)]
    if after is not None:
        got, after = lax.optimization_barrier((got, after))
    for part in got:
        total = total + part.astype(f32)
    total = total.astype(bf16)
    return total if after is None else (total, after)


def spread_of(core):
    block = jnp.arange(192, dtype=i32) // 12
    inner = jnp.arange(192, dtype=i32) % 12
    pair = jnp.where(core == 0, block, (block % 2) * SIDE + block // 2)
    source = 24 * pair + 12 * core + inner
    return hot(jnp.arange(384, dtype=i32)[:, None], source[None, :])


def on_device(queries, keys, values, segment, repack, proj, student_states, target_row):
    rows = queries.shape[0]
    devices = lax.axis_size("seq")
    shares = lax.axis_size("tp")
    core = lax.axis_index("seq") % 2
    tp_index = lax.axis_index("tp")
    place = jnp.stack([core, tp_index]).astype(i32)
    feats = proj.shape[0]
    row_ids = jnp.arange(rows, dtype=i32)
    near = exchange(to_all(proj, SIDE), NEAR).reshape(SIDE * feats, -1)
    packed = packed_rows(keys, values, segment)
    one_before = passed_along(packed, "seq", 1)
    two_before = passed_along(packed, "seq", 2)
    queries, near, place = lax.optimization_barrier((queries, near, place))
    half_proj = exchange(to_all(near, SIDE), FAR).reshape(SIDE * SIDE * feats, -1)
    attended = attend(queries, two_before, one_before, packed)
    partner = other_core(attended)
    target_dev = repack // rows
    local_slot = repack - target_dev * rows
    bucket_row = target_dev * GROUP_ROWS + row_ids % GROUP_ROWS
    pick = hot(jnp.arange(devices * GROUP_ROWS, dtype=i32)[:, None], bucket_row[None, :])
    slot_lanes = jnp.broadcast_to(local_slot.astype(bf16)[:, None], (rows, 128))
    wide = jnp.concatenate([attended, slot_lanes], 1)
    buckets = dot(pick, wide, ((1,), (0,))).astype(bf16)
    buckets = buckets.reshape(devices // 2, 2 * GROUP_ROWS, -1)
    mine, theirs = spread_of(core), spread_of(1 - core)
    target_own, target_other = targets_of(target_row, student_states, mine, theirs)
    target_other = other_core(target_other)
    buckets, half_proj, partner, target_own, target_other = lax.optimization_barrier(
        (buckets, half_proj, partner, target_own, target_other)
    )
    arrived = exchange(buckets, SAME_CORE)
    y_split = project(place, attended, partner, half_proj, False)
    y_teacher = summed_share(y_split)
    parts = [y_teacher]
    for distance in range(1, shares):
        parts.append(lax.ppermute(y_teacher, "tp", share_route(distance)))
    arrived, parts[1] = lax.optimization_barrier((arrived, parts[1]))
    own = placed_rows(arrived)
    other = other_core(own)
    targets = (target_own, target_other)
    term = term_of(place, parts, targets, attended, partner, own, other)
    far = exchange(term, FAR)
    y_split = project(place, own, other, half_proj, True)
    y_rows, far = summed_share(y_split, far)
    y_rows = y_rows.reshape(-1, 2 * rows)
    far = jnp.sum(far.astype(f32), axis=0).astype(bf16)
    last = exchange(far.reshape(SIDE, feats, -1), NEAR)
    norm_factor = 1.0 / math.sqrt(rows * devices)
    grad = jnp.sum(last.astype(f32), axis=0) * norm_factor
    first, second = y_rows[:, :rows], y_rows[:, rows:]
    rest = other_core(jnp.where(core == 0, second, first))
    out_rows = dot(jnp.where(core == 0, first, second), mine, ((0,), (1,)))
    out_rows = (out_rows + dot(rest, theirs, ((0,), (1,)))).astype(bf16)
    return (out_rows, grad)


def solution(mesh):
    placed = (
        P("seq", "tp"),
        P("seq", "tp"),
        P("seq", "tp"),
        P("seq"),
        P("seq"),
        P("seq", "tp"),
        P("seq", None),
        P("seq"),
    )
    return jax.shard_map(
        on_device,
        mesh=mesh,
        in_specs=placed,
        out_specs=(P("seq", "tp"), P("seq", "tp")),
        check_vma=False,
    )
```

```python
import functools
import math

import jax
import jax.numpy as jnp
from jax import lax
from jax.experimental import pallas as pl
from jax.experimental.pallas import tpu as pltpu
from jax.sharding import PartitionSpec as P


HEADS = 32
KV_HEADS = 4
HEAD_DIM = 128
REACH = 2
GROUP_ROWS = 4
SIDE = 8

VMEM = pl.BlockSpec(memory_space=pltpu.VMEM)
SMEM = pl.BlockSpec(memory_space=pltpu.SMEM)

neg_large = -1e30
bf16, f32, i32 = jnp.bfloat16, jnp.float32, jnp.int32


def seq_index(z, y, core):
    return (z * SIDE + y) * 2 + core


NEAR = [[seq_index(z, y, 0) for y in range(SIDE)] for z in range(SIDE)] + [
    [seq_index(z, y, 1) for z in range(SIDE)] for y in range(SIDE)
]
FAR = [[seq_index(z, y, 0) for z in range(SIDE)] for y in range(SIDE)] + [
    [seq_index(z, y, 1) for y in range(SIDE)] for z in range(SIDE)
]


SAME_CORE = [
    [seq_index(z, y, core) for z in range(SIDE) for y in range(SIDE)] for core in range(2)
]


def exchange(block, groups=None, axis="seq"):
    return lax.all_to_all(
        block, axis, split_axis=0, concat_axis=0, tiled=True, axis_index_groups=groups
    )


def passed_along(block, axis, distance):
    devices = range(lax.axis_size(axis))
    route = [(i - distance, i) for i in devices if i - distance in devices]
    return lax.ppermute(block, axis, route)


def other_core(block):
    return lax.ppermute(block, "seq", [(i, i ^ 1) for i in range(lax.axis_size("seq"))])


def to_all(block, count):
    return jnp.broadcast_to(block[None], (count,) + block.shape)


def attend_kernel(q_any, b2_ref, b1_ref, b0_ref, o_ref, bias_ref, q_ref, sem):
    load = pltpu.make_async_copy(q_any, q_ref, sem)
    load.start()
    rows = q_ref.shape[0]
    blocks = (b2_ref, b1_ref, b0_ref)
    seg_lanes = [
        b[2 * rows + i : 2 * rows + i + 1, :].astype(f32) for b in blocks for i in range(2)
    ]
    seg_keys = jnp.concatenate(seg_lanes, axis=1)
    for i in range(2):
        column = jnp.transpose(jnp.broadcast_to(seg_lanes[4 + i], (HEAD_DIM, HEAD_DIM)))
        column = jnp.concatenate([column] * 6, axis=1)
        row_pos = lax.broadcasted_iota(i32, column.shape, 0) + i * HEAD_DIM
        key_pos = lax.broadcasted_iota(i32, column.shape, 1) - REACH * rows
        allowed = (column == seg_keys) & (key_pos <= row_pos)
        bias_ref[pl.ds(i * HEAD_DIM, HEAD_DIM), :] = jnp.where(allowed, 0.0, neg_large)
    keys = jnp.concatenate([b[0:rows, :] for b in blocks], axis=0)
    values = jnp.concatenate([b[rows : 2 * rows, :] for b in blocks], axis=0)
    scale = 1.0 / math.sqrt(HEAD_DIM)
    load.wait()
    for head in range(HEADS // KV_HEADS):
        lanes = slice(head * HEAD_DIM, (head + 1) * HEAD_DIM)
        scores = dot(q_ref[:, lanes], keys, ((1,), (1,))) * scale + bias_ref[...]
        top = jnp.max(scores, axis=-1, keepdims=True)
        expo = jnp.exp(scores - top)
        weights = (expo * (1.0 / jnp.sum(expo, axis=-1, keepdims=True))).astype(bf16)
        o_ref[:, lanes] = dot(weights, values, ((1,), (0,))).astype(bf16)


def packed_rows(keys, values, segment):
    lanes = keys.shape[1]
    seg_rows = (segment + 1).astype(bf16).reshape(-1, lanes)
    seg_rows = jnp.concatenate([seg_rows, jnp.zeros((14, lanes), bf16)], 0)
    return jnp.concatenate([keys, values, seg_rows], 0)


def attend(queries, two_before, one_before, packed):
    rows = queries.shape[0]
    return pl.pallas_call(
        attend_kernel,
        out_shape=jax.ShapeDtypeStruct(queries.shape, bf16),
        in_specs=[pl.BlockSpec(memory_space=pl.ANY)] + [VMEM] * 3,
        out_specs=VMEM,
        scratch_shapes=[
            pltpu.VMEM((rows, (REACH + 1) * rows), f32),
            pltpu.VMEM(queries.shape, bf16),
            pltpu.SemaphoreType.DMA,
        ],
        compiler_params=pltpu.CompilerParams(vmem_limit_bytes=24 << 20),
        cost_estimate=pl.CostEstimate(
            flops=4 * rows * 3 * rows * 1024, bytes_accessed=2 << 20, transcendentals=rows * 3 * rows * 8
        ),
        name="attend",
    )(queries, two_before, one_before, packed)


def dot(a, b, dims):
    return lax.dot_general(a, b, (dims, ((), ())), preferred_element_type=f32)


def hot(a, b):
    return (a == b).astype(bf16)


def chunk_of(core, ring, quarter):
    return jnp.where(core == 0, ring * 4 + quarter, quarter * SIDE + ring)


def place_kernel(in_ref, out_ref):
    count = out_ref.shape[0]
    arrived = in_ref[...].reshape(count, -1)
    slot = arrived[:, 1024:].astype(f32)
    row = lax.broadcasted_iota(i32, slot.shape, 0)
    owner = lax.rem(row, 2 * GROUP_ROWS) // GROUP_ROWS
    slot = slot + (owner * (count // 2)).astype(f32)
    slot = jnp.concatenate([slot] * (count // 128), axis=1)
    slot_hot = (slot == lax.broadcasted_iota(i32, slot.shape, 1).astype(f32)).astype(bf16)
    out_ref[...] = dot(slot_hot, arrived[:, :1024], ((0,), (0,))).astype(bf16)


def placed_rows(arrived):
    count = arrived.shape[0] * arrived.shape[1]
    return pl.pallas_call(
        place_kernel,
        out_shape=jax.ShapeDtypeStruct((count, 1024), bf16),
        in_specs=[VMEM],
        out_specs=VMEM,
        compiler_params=pltpu.CompilerParams(vmem_limit_bytes=16 << 20),
        cost_estimate=pl.CostEstimate(
            flops=2 * count * count * 1024, bytes_accessed=3 << 20, transcendentals=0
        ),
        name="place",
    )(arrived)


def project_kernel(add, place_ref, own_ref, other_ref, proj_ref, out_ref):
    core, share = place_ref[0], place_ref[1]
    if add:
        both = own_ref[...] + other_ref[...]
    else:
        both = jnp.concatenate([own_ref[...], other_ref[...]], axis=0)
    for ring in range(SIDE):
        y = dot(proj_ref[ring * 96 : ring * 96 + 96], both, ((1,), (1,))).astype(bf16)
        for quarter in range(4):
            chunk = chunk_of(core, ring, quarter)
            away = lax.rem(chunk // 8 - share + 4, 4)
            out_ref[away, lax.rem(chunk, 8)] = y[quarter * 24 : quarter * 24 + 24]


def project(place, own, other, half_proj, add):
    feats = own.shape[1]
    rows = own.shape[0] if add else 2 * own.shape[0]
    return pl.pallas_call(
        functools.partial(project_kernel, add),
        out_shape=jax.ShapeDtypeStruct((4, 8, 24, rows), bf16),
        in_specs=[SMEM] + [VMEM] * 3,
        out_specs=VMEM,
        compiler_params=pltpu.CompilerParams(vmem_limit_bytes=(56 if add else 16) << 20),
        cost_estimate=pl.CostEstimate(
            flops=2 * 768 * rows * feats, bytes_accessed=4 << 20, transcendentals=0
        ),
    )(place, own, other, half_proj)


def targets_kernel(row_ref, states_ref, mine_ref, theirs_ref, own_ref, other_ref):
    rows = states_ref.shape[0]
    source = lax.broadcasted_iota(i32, (rows, rows), 0)
    chosen = jnp.where(source == row_ref[...], 1.0, 0.0).astype(bf16)
    for spread_ref, out_ref in ((mine_ref, own_ref), (theirs_ref, other_ref)):
        for share in range(4):
            states = states_ref[:, share * 384 : share * 384 + 384]
            part = dot(spread_ref[...], states, ((0,), (1,))).astype(bf16)
            part = dot(part, chosen, ((1,), (0,))).astype(bf16)
            for quarter in range(8):
                out_ref[share * 8 + quarter] = part[quarter * 24 : quarter * 24 + 24]


def targets_of(target_row, student_states, mine, theirs):
    rows = student_states.shape[0]
    out = jax.ShapeDtypeStruct((32, 24, rows), bf16)
    return pl.pallas_call(
        targets_kernel,
        out_shape=(out, out),
        in_specs=[VMEM] * 4,
        out_specs=(VMEM, VMEM),
        compiler_params=pltpu.CompilerParams(vmem_limit_bytes=16 << 20),
        cost_estimate=pl.CostEstimate(
            flops=2 * 1536 * rows * (384 + 256), bytes_accessed=2 << 20, transcendentals=0
        ),
        name="targets",
    )(target_row.reshape(1, rows), student_states, mine, theirs)


def term_kernel(place_ref, *refs):
    parts, refs = refs[:4], refs[4:]
    own_t, other_t, own_ref, other_ref, own_m, other_m, out_ref, held, moved = refs
    core, share = place_ref[0], place_ref[1]
    half = own_t.shape[2]
    for i, part in enumerate(parts):
        held[i] = part[...]
    attended = jnp.concatenate([own_ref[...], other_ref[...]], axis=0)
    moved[...] = own_m[...] + other_m[...]
    right = [moved[pl.ds(c * half, half), :] for c in (core, 1 - core)]
    for ring in range(SIDE):
        chunks = [chunk_of(core, ring, quarter) for quarter in range(4)]
        left = [held[lax.rem(share - k // 8 + 4, 4), lax.rem(k, 8)] for k in chunks]
        total = dot(jnp.concatenate(left, axis=0), attended, ((1,), (0,)))
        for target_ref, rows in zip((own_t, other_t), right):
            left = jnp.concatenate([target_ref[k] for k in chunks], axis=0)
            total = total - dot(left, rows, ((1,), (0,)))
        out_ref[ring] = total.astype(bf16)


def term_of(place, parts, targets, own, other, own_m, other_m):
    rows, feats = own_m.shape
    return pl.pallas_call(
        term_kernel,
        out_shape=jax.ShapeDtypeStruct((SIDE, 96, feats), bf16),
        in_specs=[SMEM] + [VMEM] * 10,
        out_specs=VMEM,
        scratch_shapes=[pltpu.VMEM((4, 8, 24, rows), bf16), pltpu.VMEM((rows, feats), bf16)],
        compiler_params=pltpu.CompilerParams(vmem_limit_bytes=56 << 20),
        cost_estimate=pl.CostEstimate(
            flops=4 * 768 * rows * feats, bytes_accessed=8 << 20, transcendentals=0
        ),
        name="term",
    )(place, *parts, *targets, own, other, own_m, other_m)


def share_route(distance):
    return [(i, (i + distance) % 4) for i in range(4)]


def summed_share(y_split):
    got = [lax.ppermute(y_split[k], "tp", share_route(k)) for k in range(1, 4)]
    total = y_split[0].astype(f32)
    for part in got:
        total = total + part.astype(f32)
    return total.astype(bf16)


def spread_of(core):
    block = jnp.arange(192, dtype=i32) // 12
    inner = jnp.arange(192, dtype=i32) % 12
    pair = jnp.where(core == 0, block, (block % 2) * SIDE + block // 2)
    source = 24 * pair + 12 * core + inner
    return hot(jnp.arange(384, dtype=i32)[:, None], source[None, :])


def on_device(queries, keys, values, segment, repack, proj, student_states, target_row):
    rows = queries.shape[0]
    devices = lax.axis_size("seq")
    shares = lax.axis_size("tp")
    core = lax.axis_index("seq") % 2
    tp_index = lax.axis_index("tp")
    place = jnp.stack([core, tp_index]).astype(i32)
    feats = proj.shape[0]
    row_ids = jnp.arange(rows, dtype=i32)
    near = exchange(to_all(proj, SIDE), NEAR).reshape(SIDE * feats, -1)
    packed = packed_rows(keys, values, segment)
    one_before = passed_along(packed, "seq", 1)
    two_before = passed_along(packed, "seq", 2)
    queries, near, place = lax.optimization_barrier((queries, near, place))
    half_proj = exchange(to_all(near, SIDE), FAR).reshape(SIDE * SIDE * feats, -1)
    attended = attend(queries, two_before, one_before, packed)
    partner = other_core(attended)
    target_dev = repack // rows
    local_slot = repack - target_dev * rows
    bucket_row = target_dev * GROUP_ROWS + row_ids % GROUP_ROWS
    pick = hot(jnp.arange(devices * GROUP_ROWS, dtype=i32)[:, None], bucket_row[None, :])
    slot_lanes = jnp.broadcast_to(local_slot.astype(bf16)[:, None], (rows, 128))
    wide = jnp.concatenate([attended, slot_lanes], 1)
    buckets = dot(pick, wide, ((1,), (0,))).astype(bf16)
    buckets = buckets.reshape(devices // 2, 2 * GROUP_ROWS, -1)
    mine, theirs = spread_of(core), spread_of(1 - core)
    target_own, target_other = targets_of(target_row, student_states, mine, theirs)
    target_other = other_core(target_other)
    buckets, half_proj, partner, target_own, target_other = lax.optimization_barrier(
        (buckets, half_proj, partner, target_own, target_other)
    )
    arrived = exchange(buckets, SAME_CORE)
    y_split = project(place, attended, partner, half_proj, False)
    y_teacher = summed_share(y_split)
    parts = [y_teacher]
    for distance in range(1, shares):
        parts.append(lax.ppermute(y_teacher, "tp", share_route(distance)))
    arrived, parts[0] = lax.optimization_barrier((arrived, parts[0]))
    own = placed_rows(arrived)
    other = other_core(own)
    targets = (target_own, target_other)
    term = term_of(place, parts, targets, attended, partner, own, other)
    far = exchange(term, FAR)
    y_split = project(place, own, other, half_proj, True)
    y_rows = summed_share(y_split)
    y_rows = y_rows.reshape(-1, 2 * rows)
    far = jnp.sum(far.astype(f32), axis=0).astype(bf16)
    last = exchange(far.reshape(SIDE, feats, -1), NEAR)
    norm_factor = 1.0 / math.sqrt(rows * devices)
    grad = jnp.sum(last.astype(f32), axis=0) * norm_factor
    first, second = y_rows[:, :rows], y_rows[:, rows:]
    rest = other_core(jnp.where(core == 0, second, first))
    out_rows = dot(jnp.where(core == 0, first, second), mine, ((0,), (1,)))
    out_rows = (out_rows + dot(rest, theirs, ((0,), (1,)))).astype(bf16)
    return (out_rows, grad)


def solution(mesh):
    placed = (
        P("seq", "tp"),
        P("seq", "tp"),
        P("seq", "tp"),
        P("seq"),
        P("seq"),
        P("seq", "tp"),
        P("seq", None),
        P("seq"),
    )
    return jax.shard_map(
        on_device,
        mesh=mesh,
        in_specs=placed,
        out_specs=(P("seq", "tp"), P("seq", "tp")),
        check_vma=False,
    )
```
